256 devices in a mesh: tower: 64 (over x, y, z_hi, core), member: 4 (over z_lo).
Axes of the slice: x: 4, y: 4, z: 8 (z_hi: 2, z_lo: 4; z = z_hi * 4 + z_lo), core: 2. Of those that a mesh axis runs over, the one named last changes fastest.
Arguments:
- slabs: bfloat16 [64, 1024, 4096], P('tower', None, 'member'), may hold values from -6 to 6
- cross_down: bfloat16 [64, 2, 4096, 512], P('tower', None, None, 'member'), may hold values from -0.09375 to 0.09375
- cross_up: bfloat16 [64, 2, 4096, 512], P('tower', None, None, 'member'), may hold values from -0.25 to 0.25
- cross_bias: float32 [64, 2, 4096], P('tower'), may hold values from -3 to 3
- projector: bfloat16 [64, 4096, 256], P('tower'), may hold values from -0.09375 to 0.09375
- placement: int32 [64, 32], P('tower'), may hold values from 0 to 31, each once within a row
- owner: int32 [4, 256], replicated, may hold values from 0 to 255, each once within a row
- inter_grad: bfloat16 [1024, 16384], P(('tower', 'member')), may hold values from -6 to 6
Outputs:
- interactions: float32 [1024, 16384], P(('tower', 'member'))
- slab_grad: bfloat16 [64, 1024, 4096], P('tower', None, 'member')
The draws below stay inside these ranges and needn't reach their ends.
Inputs may be any that keep to these rules, and one draw needn't show every extreme that they name: Each row of placement names every feature of its tower once. Each row of owner names every sample of its block once.
All inputs are finite; a program needn't handle non-finite values.
Results may differ from the reference program's by a relative error of at most 0.018.
Values may be sent and summed in bfloat16 or wider, within the bound.
A program may use at most 128 MiB of HBM per device.

```python
import jax
import jax.numpy as jnp
from jax import lax

EMB = 128
FEATS = 32
RANK = 512
VECS = 128
LAYERS = 2
ROWS = 256
WIDTH = 4096
TOWERS = 64
MEMBERS = 4
SAMPLES = 1024
OWNED = 4
TOWER_OUT = 256


def block_scale(stream_key, dims, split, smallest, high):
    def one(dim, parts):
        heights = jax.random.uniform(jax.random.fold_in(jax.random.fold_in(stream_key, 6), dim), (parts,), jnp.float32, smallest / len(split), high / len(split))
        return jnp.repeat(jnp.exp(heights), dims[dim] // parts).reshape((-1,) + (1,) * (len(dims) - dim - 1))

    loudness = one(*split[0])
    for cut in split[1:]:
        loudness = loudness * one(*cut)
    return loudness


def scatter_about(own_key, dims, deviation, limit, split=(), kind=jnp.bfloat16):
    factor_of = block_scale(own_key, dims, split, -0.22, 0.18) if split else 1.0
    drawn = jax.random.normal(own_key, dims, jnp.float32) * deviation * factor_of
    return jnp.minimum(jnp.maximum(drawn, -limit), limit).astype(kind)


def setup_inputs(seed: int = 0) -> dict:
    seeds = jax.random.split(jax.random.key(seed), 9)
    return {
        "slabs": scatter_about(seeds[0], (TOWERS, SAMPLES, WIDTH), 1.0, 6.0, ((0, 64), (2, 4))),
        "cross_down": scatter_about(seeds[1], (TOWERS, LAYERS, WIDTH, RANK), WIDTH ** -0.5, 0.09375, ((0, 64), (3, 4))),
        "cross_up": scatter_about(seeds[2], (TOWERS, LAYERS, WIDTH, RANK), RANK ** -0.5, 0.25, ((0, 64), (3, 4))),
        "cross_bias": scatter_about(seeds[3], (TOWERS, LAYERS, WIDTH), 0.5, 3.0, ((0, 64),), jnp.float32),
        "projector": scatter_about(seeds[4], (TOWERS, WIDTH, TOWER_OUT), WIDTH ** -0.5, 0.09375, ((0, 64),)),
        "placement": jax.vmap(lambda own: jax.random.permutation(own, FEATS))(jax.random.split(seeds[5], TOWERS)).reshape((TOWERS, FEATS)).astype(jnp.int32),
        "owner": jax.vmap(lambda own: jax.random.permutation(own, ROWS))(jax.random.split(seeds[6], MEMBERS)).reshape((MEMBERS, ROWS)).astype(jnp.int32),
        "inter_grad": scatter_about(seeds[7], (SAMPLES, VECS * VECS), 1.0, 6.0, ((0, 256),)),
    }


def tower_forward(inputs, downs, ups, biases, projection):
    current = inputs
    start_f = inputs.astype(jnp.float32)
    scales = []
    for depth in range(LAYERS):
        hidden = jnp.dot(current, downs[depth], preferred_element_type=jnp.float32).astype(jnp.bfloat16)
        scale_now = jnp.dot(hidden, ups[depth].T, preferred_element_type=jnp.float32) + biases[depth]
        scales.append(scale_now)
        current = (start_f * scale_now + current.astype(jnp.float32)).astype(jnp.bfloat16)
    vector = jnp.dot(current, projection, preferred_element_type=jnp.float32).astype(jnp.bfloat16)
    return vector, scales


def placed(slab, order):
    return slab.reshape(SAMPLES, FEATS, EMB)[:, order].reshape(SAMPLES, WIDTH)


def reference(slabs, cross_down, cross_up, cross_bias, projector, placement, owner, inter_grad):
    def forward_one(items):
        slab, downs, ups, biases, projection, order = items
        vector, scales = tower_forward(placed(slab, order), downs, ups, biases, projection)
        return vector

    vectors = lax.map(forward_one, (slabs, cross_down, cross_up, cross_bias, projector, placement))
    per_sample = jnp.transpose(vectors, (1, 0, 2)).reshape(SAMPLES, VECS, EMB).astype(jnp.float32)
    table = jnp.einsum('bie,bje->bij', per_sample, per_sample) / EMB
    position = jnp.arange(SAMPLES, dtype=jnp.int32)
    block = position // OWNED
    tower_of = block // MEMBERS
    member_of = block % MEMBERS
    local = tower_of * OWNED + position % OWNED
    index = (member_of * ROWS + owner[member_of, local]).astype(jnp.int32)
    interactions = table.reshape(SAMPLES, VECS * VECS)[index]
    cotangent = jnp.zeros((SAMPLES, VECS * VECS), jnp.float32).at[index].set(inter_grad.astype(jnp.float32))
    cotangent = cotangent.reshape(SAMPLES, VECS, VECS)
    symmetric = cotangent + jnp.swapaxes(cotangent, 1, 2)
    vec_grad = (jnp.einsum('bij,bje->bie', symmetric, per_sample) / EMB).astype(jnp.bfloat16)
    per_tower = jnp.transpose(vec_grad.reshape(SAMPLES, TOWERS, TOWER_OUT), (1, 0, 2))

    def backward_one(items):
        slab, downs, ups, biases, projection, order, vector_grad = items
        inputs = placed(slab, order)
        vector, scales = tower_forward(inputs, downs, ups, biases, projection)
        inputs_f = inputs.astype(jnp.float32)
        gradient = jnp.dot(vector_grad, projection.T, preferred_element_type=jnp.float32)
        accum = jnp.zeros((SAMPLES, WIDTH), jnp.float32)
        for depth in reversed(range(LAYERS)):
            accum = accum + gradient * scales[depth]
            dscale = (gradient * inputs_f).astype(jnp.bfloat16)
            dhidden = jnp.dot(dscale, ups[depth], preferred_element_type=jnp.float32).astype(jnp.bfloat16)
            gradient = gradient + jnp.dot(dhidden, downs[depth].T, preferred_element_type=jnp.float32)
        total = (gradient + accum).astype(jnp.bfloat16)
        inverse = jnp.argsort(order).astype(jnp.int32)
        return total.reshape(SAMPLES, FEATS, EMB)[:, inverse].reshape(SAMPLES, WIDTH)

    slab_grad = lax.map(backward_one, (slabs, cross_down, cross_up, cross_bias, projector, placement, per_tower))
    return interactions, slab_grad
```

```python
import functools

import jax
import jax.numpy as jnp
from jax import lax
from jax.experimental import pallas as pl
from jax.experimental.pallas import tpu as pltpu
from jax.sharding import PartitionSpec as P

F32 = jnp.float32
BF16 = jnp.bfloat16
E = 128
N = 4
NB = 256
NT = (((1,), (1,)), ((), ()))


def dot(a, b):
    return jnp.dot(a, b, preferred_element_type=F32)


def dot_t(a, b):
    return lax.dot_general(a, b, NT, preferred_element_type=F32)


def line_position():
    me = lax.axis_index("member")
    near = me + 1 - 2 * (me % 2)
    hub = ((me + 1) // 2) % 2
    return me, near, 3 - me, hub


def greet(me):
    barrier = pltpu.get_barrier_semaphore()
    for d in range(1, N):
        pl.semaphore_signal(barrier, inc=1, device_id={"member": (me + d) % N})
    pl.semaphore_wait(barrier, N - 1)


class LineSum:
    def __init__(self, block, total, own, part, from_end, side, from_side, sems):
        self.me, self.near, self.across, self.hub = line_position()
        self.block, self.total, self.own = block, total, own
        self.part, self.from_end, self.side, self.from_side = part, from_end, side, from_side
        self.sems = sems

    def rows(self, c):
        return pl.ds(pl.multiple_of(c * self.block, self.block), self.block)

    def copy(self, kind, src, dst, layer, c, peer):
        rows = self.rows(c)
        return pltpu.make_async_remote_copy(
            src_ref=src.at[layer, rows],
            dst_ref=dst.at[layer, rows],
            send_sem=self.sems.at[2 * kind, layer, c],
            recv_sem=self.sems.at[2 * kind + 1, layer, c],
            device_id={"member": peer},
        )

    def to_hub(self, layer, c):
        return self.copy(0, self.part, self.from_end, layer, c, self.near)

    def to_side(self, layer, c):
        return self.copy(1, self.side, self.from_side, layer, c, self.across)

    def to_end(self, layer, c):
        return self.copy(2, self.total, self.total, layer, c, self.near)

    def put(self, layer, c, value):
        @pl.when(self.hub == 1)
        def _():
            self.own[self.rows(c), :] = value

        @pl.when(self.hub == 0)
        def _():
            self.part[layer, self.rows(c), :] = value.astype(BF16)
            self.to_hub(layer, c).start()

    def exchange(self, layer, c):
        rows = self.rows(c)

        @pl.when(self.hub == 1)
        def _():
            self.to_hub(layer, c).wait_recv()
            both = self.own[rows, :] + self.from_end[layer, rows, :].astype(F32)
            self.side[layer, rows, :] = both.astype(BF16)
            self.to_side(layer, c).start()

    def get(self, layer, c):
        rows = self.rows(c)

        @pl.when(self.hub == 1)
        def _():
            self.to_side(layer, c).wait_recv()
            whole = self.side[layer, rows, :].astype(F32) + self.from_side[layer, rows, :].astype(F32)
            self.total[layer, rows, :] = whole.astype(BF16)
            self.to_end(layer, c).start()

        @pl.when(self.hub == 0)
        def _():
            self.to_end(layer, c).wait_recv()

    def drain(self, layer, c):
        @pl.when(self.hub == 1)
        def _():
            self.to_side(layer, c).wait_send()
            self.to_end(layer, c).wait_send()

        @pl.when(self.hub == 0)
        def _():
            self.to_hub(layer, c).wait_send()


def each(count, body):
    lax.fori_loop(0, count, lambda i, _: (body(i), 0)[1], 0)


def ranks(w_ref, k, lo, rows):
    return jnp.concatenate([w_ref[k, r, lo : lo + rows, :] for r in range(N)], axis=1)


def times_down(a, w_ref, k):
    width = w_ref.shape[2]
    halves = []
    for j in range(0, N, 2):
        right = jnp.concatenate([w_ref[k, j], w_ref[k, j + 1]], axis=1)
        halves.append(dot(a, right))
    return jnp.concatenate(halves, axis=1)


def forward_kernel(
    inv_ref, own_ref, x_ref, down_ref, up_ref, bias_ref, proj_ref,
    ordered_ref, w_ref, pw_ref, h_ref, bw_ref,
    stage, cur, own, part, from_end, side, from_side, v_out, v_own, v_in,
    sems, w_sems, v_sems,
):
    samples, width = x_ref.shape
    block = samples // N
    line = LineSum(block, h_ref, own, part, from_end, side, from_side, sems)
    me = line.me
    feats = width // E

    def send_w(k, d):
        peer = (me + d) % N
        return pltpu.make_async_remote_copy(
            src_ref=stage.at[k, peer],
            dst_ref=w_ref.at[k, me],
            send_sem=w_sems.at[0, k, peer],
            recv_sem=w_sems.at[1, k, me],
            device_id={"member": peer},
        )

    def recv_w(k, d):
        peer = (me + d) % N
        return pltpu.make_async_remote_copy(
            src_ref=stage.at[k, peer],
            dst_ref=w_ref.at[k, peer],
            send_sem=w_sems.at[0, k, peer],
            recv_sem=w_sems.at[1, k, peer],
            device_id={"member": peer},
        )

    def stage_w(k):
        source = down_ref if k % 2 == 0 else up_ref

        def one(f):
            at = pl.multiple_of((f % feats) * E, E)
            stage[k, f // feats, pl.ds(at, E), :] = source[k // 2, inv_ref[f]]

        each(N * feats, one)
        w_ref[k, me] = stage[k, me]

    def start_w(k):
        for d in range(1, N):
            send_w(k, d).start()

    def sent_w(k):
        for d in range(1, N):
            send_w(k, d).wait_send()

    def got_w(k):
        for d in range(1, N):
            recv_w(k, d).wait_recv()

    greet(me)
    stage_w(0)
    start_w(0)
    for k in range(1, 4):
        stage_w(k)
    for i in range(feats):
        slot = inv_ref[me * feats + i]
        pw_ref[i * E : (i + 1) * E, :] = proj_ref[slot]
        for layer in range(2):
            bw_ref[layer, :, i * E : (i + 1) * E] = bias_ref[layer, slot]
    sent_w(0)
    start_w(1)
    got_w(0)
    each(N, lambda c: line.put(0, c, times_down(x_ref[line.rows(c), :], w_ref, 0)))
    each(N, lambda c: line.exchange(0, c))
    sent_w(1)
    start_w(2)
    each(N, lambda c: line.get(0, c))
    got_w(1)

    def next_current(layer, c):
        rows = line.rows(c)
        hidden = h_ref[layer, rows, :]
        for lo in range(0, width, NB):
            cols = slice(lo, lo + NB)
            scale = dot_t(hidden, ranks(w_ref, 2 * layer + 1, lo, NB)) + bw_ref[layer, :, cols]
            x = x_ref[rows, cols].astype(F32)
            before = x if layer == 0 else cur[rows, cols].astype(F32)
            cur[rows, cols] = (x * scale + before).astype(BF16)

    each(N, lambda c: next_current(0, c))
    sent_w(2)
    start_w(3)
    got_w(2)
    each(N, lambda c: line.put(1, c, times_down(cur[line.rows(c), :], w_ref, 2)))
    each(N, lambda c: line.exchange(1, c))
    each(N, lambda c: line.get(1, c))
    got_w(3)

    def v_copy(slot, peer):
        return pltpu.make_async_remote_copy(
            src_ref=v_out.at[peer],
            dst_ref=v_in.at[slot],
            send_sem=v_sems.at[0, peer],
            recv_sem=v_sems.at[1, slot],
            device_id={"member": peer},
        )

    def vectors(c):
        next_current(1, c)
        part_v = dot(cur[line.rows(c), :], pw_ref[...])

        @pl.when(c == me)
        def _():
            v_own[...] = part_v

        @pl.when(c != me)
        def _():
            v_out[c] = part_v.astype(BF16)
            v_copy(me, c).start()

    each(N, vectors)
    vector = v_own[...]
    for d in range(1, N):
        peer = (me + d) % N
        v_copy(peer, peer).wait_recv()
        vector = vector + v_in[peer].astype(F32)
    vector = vector.astype(BF16)
    shape = (2 * block, block)
    hit = own_ref[...] == lax.broadcasted_iota(jnp.int32, shape, 1)
    odd = lax.broadcasted_iota(jnp.int32, shape, 0) % 2
    total = jnp.zeros((2 * block, E), F32)
    for k in range(2):
        pick = jnp.where(hit & (odd == k), 1.0, 0.0).astype(BF16)
        total = total + dot(pick, vector[:, k * E : (k + 1) * E])
    ordered_ref[...] = total.astype(BF16)

    sent_w(3)
    for d in range(1, N):
        v_copy(me, (me + d) % N).wait_send()
    for layer in range(2):
        each(N, lambda c: line.drain(layer, c))


def backward_kernel(
    own_ref, ret_ref, x_ref, w_ref, pw_ref, h_ref, bw_ref,
    out_ref,
    vg, grad, scales, own, part, from_end, side, from_side, dh,
    sems, v_sems,
):
    samples, width = x_ref.shape
    block = samples // N
    line = LineSum(block, dh, own, part, from_end, side, from_side, sems)
    me = line.me
    greet(me)

    shape = (block, 2 * block)
    hit = own_ref[...] == lax.broadcasted_iota(jnp.int32, shape, 0)
    odd = lax.broadcasted_iota(jnp.int32, shape, 1) % 2
    for k in range(2):
        pick = jnp.where(hit & (odd == k), 1.0, 0.0).astype(BF16)
        vg[me, :, k * E : (k + 1) * E] = dot(pick, ret_ref[...]).astype(BF16)

    def v_copy(slot, peer):
        return pltpu.make_async_remote_copy(
            src_ref=vg.at[slot],
            dst_ref=vg.at[slot],
            send_sem=v_sems.at[0, peer],
            recv_sem=v_sems.at[1, slot],
            device_id={"member": peer},
        )

    for d in range(1, N):
        v_copy(me, (me + d) % N).start()

    def scale_of(c):
        rows = line.rows(c)
        for layer in range(2):
            hidden = h_ref[layer, rows, :]
            for lo in range(0, width, NB):
                cols = slice(lo, lo + NB)
                scale = dot_t(hidden, ranks(w_ref, 2 * layer + 1, lo, NB)) + bw_ref[layer, :, cols]
                scales[layer, rows, cols] = scale

    each(N, scale_of)
    for d in range(1, N):
        v_copy((me + d) % N, (me + d) % N).wait_recv()

    def last_layer(c):
        rows = line.rows(c)
        total = jnp.zeros((block, w_ref.shape[1] * w_ref.shape[3]), F32)
        for lo in range(0, width, NB):
            cols = slice(lo, lo + NB)
            g = dot_t(vg[c], pw_ref[cols, :])
            grad[rows, cols] = g
            dscale = (g * x_ref[rows, cols].astype(F32)).astype(BF16)
            total = total + dot(dscale, ranks(w_ref, 3, lo, NB))
        line.put(0, c, total)

    each(N, last_layer)
    each(N, lambda c: line.exchange(0, c))

    def first_layer(c):
        rows = line.rows(c)
        line.get(0, c)
        dhidden = dh[0, rows, :]
        total = jnp.zeros((block, w_ref.shape[1] * w_ref.shape[3]), F32)
        for lo in range(0, width, NB):
            cols = slice(lo, lo + NB)
            g2 = grad[rows, cols]
            g1 = g2 + dot_t(dhidden, ranks(w_ref, 2, lo, NB))
            grad[rows, cols] = g1 + (g2 * scales[1, rows, cols] + g1 * scales[0, rows, cols])
            dscale = (g1 * x_ref[rows, cols].astype(F32)).astype(BF16)
            total = total + dot(dscale, ranks(w_ref, 1, lo, NB))
        line.put(1, c, total)

    each(N, first_layer)
    each(N, lambda c: line.exchange(1, c))

    def finish(c):
        rows = line.rows(c)
        line.get(1, c)
        dhidden = dh[1, rows, :]
        for lo in range(0, width, NB):
            cols = slice(lo, lo + NB)
            g0 = grad[rows, cols] + dot_t(dhidden, ranks(w_ref, 0, lo, NB))
            out_ref[rows, cols] = g0.astype(BF16)

    each(N, finish)
    for d in range(1, N):
        v_copy(me, (me + d) % N).wait_send()
    for layer in range(2):
        each(N, lambda c: line.drain(layer, c))


def line_scratch(samples, rank):
    return [pltpu.VMEM((samples, rank), F32)] + [pltpu.VMEM((2, samples, rank), BF16)] * 4


def vmem():
    return pl.BlockSpec(memory_space=pltpu.VMEM)


def params(collective_id):
    return pltpu.CompilerParams(
        collective_id=collective_id, has_side_effects=True, vmem_limit_bytes=60 << 20
    )


def per_device(slabs, cross_down, cross_up, cross_bias, projector, placement, owner, inter_grad):
    x = slabs[0]
    samples, width = x.shape
    block = samples // N
    slots = placement.shape[1]
    rank = N * cross_down.shape[3]
    towers = block // 4
    order = placement[0]
    index = jnp.arange(slots, dtype=jnp.int32)
    inverse = jnp.sum(jnp.where(order[None, :] == index[:, None], index[None, :], 0), axis=1)
    own_row = lax.dynamic_index_in_dim(owner, lax.axis_index("member"), 0, keepdims=False)
    own_twice = jnp.repeat(own_row, 2)
    sds = jax.ShapeDtypeStruct
    ordered, w, pw, hidden, bw = pl.pallas_call(
        forward_kernel,
        out_shape=(
            sds((2 * block, E), BF16),
            sds((4, N, width, E), BF16),
            sds((width, 2 * E), BF16),
            sds((2, samples, rank), BF16),
            sds((2, 1, width), F32),
        ),
        in_specs=[pl.BlockSpec(memory_space=pltpu.SMEM)] + [vmem()] * 6,
        out_specs=(vmem(),) * 5,
        scratch_shapes=[
            pltpu.VMEM((4, N, width, E), BF16),
            pltpu.VMEM((samples, width), BF16),
            *line_scratch(samples, rank),
            pltpu.VMEM((N, block, 2 * E), BF16),
            pltpu.VMEM((block, 2 * E), F32),
            pltpu.VMEM((N, block, 2 * E), BF16),
            pltpu.SemaphoreType.DMA((6, 2, N)),
            pltpu.SemaphoreType.DMA((2, 4, N)),
            pltpu.SemaphoreType.DMA((2, N)),
        ],
        compiler_params=params(0),
        name="forward",
    )(
        inverse, own_twice[:, None], x,
        cross_down[0].reshape(2, slots, E, E), cross_up[0].reshape(2, slots, E, E),
        cross_bias[0].reshape(2, slots, 1, E), projector[0].reshape(slots, E, 2 * E),
    )

    owned = lax.all_to_all(ordered.reshape(towers, 8, E), "tower", split_axis=0, concat_axis=0, tiled=True)
    vectors = owned.reshape(towers, 4, 2, E).transpose(1, 0, 2, 3).reshape(4, 2 * towers, E)
    table = jnp.einsum("bie,bje->bij", vectors, vectors, preferred_element_type=F32) / E
    interactions = table.reshape(4, -1)
    cot = inter_grad.astype(F32).reshape(4, 2 * towers, 2 * towers)
    symmetric = cot + jnp.swapaxes(cot, 1, 2)
    vec_grad = (jnp.einsum("bij,bje->bie", symmetric, vectors.astype(F32)) / E).astype(BF16)
    back = vec_grad.reshape(4, towers, 2, E).transpose(1, 0, 2, 3).reshape(towers, 8, E)
    returned = lax.all_to_all(back, "tower", split_axis=0, concat_axis=0, tiled=True)

    slab_grad = pl.pallas_call(
        backward_kernel,
        out_shape=sds((samples, width), BF16),
        in_specs=[vmem()] * 7,
        out_specs=vmem(),
        scratch_shapes=[
            pltpu.VMEM((N, block, 2 * E), BF16),
            pltpu.VMEM((samples, width), F32),
            pltpu.VMEM((2, samples, width), F32),
            *line_scratch(samples, rank),
            pltpu.VMEM((2, samples, rank), BF16),
            pltpu.SemaphoreType.DMA((6, 2, N)),
            pltpu.SemaphoreType.DMA((2, N)),
        ],
        compiler_params=params(1),
        name="backward",
    )(own_twice[None, :], returned.reshape(2 * block, E), x, w, pw, hidden, bw)
    return interactions, slab_grad[None]


def solution(mesh):
    placed = (
        P("tower", None, "member"),
        P("tower", None, None, "member"),
        P("tower", None, None, "member"),
        P("tower", None, None),
        P("tower", None, None),
        P("tower", None),
        P(),
        P(("tower", "member"), None),
    )
    return jax.shard_map(
        per_device,
        mesh=mesh,
        in_specs=placed,
        out_specs=(P(("tower", "member"), None), P("tower", None, "member")),
        check_vma=False,
    )
```

```python
import functools

import jax
import jax.numpy as jnp
from jax import lax
from jax.experimental import pallas as pl
from jax.experimental.pallas import tpu as pltpu
from jax.sharding import PartitionSpec as P

F32 = jnp.float32
BF16 = jnp.bfloat16
E = 128
N = 4
NB = 256
NT = (((1,), (1,)), ((), ()))
TN = (((0,), (0,)), ((), ()))


def dot(a, b):
    return jnp.dot(a, b, preferred_element_type=F32)


def dot_t(a, b):
    return lax.dot_general(a, b, NT, preferred_element_type=F32)


def line_position():
    me = lax.axis_index("member")
    near = me + 1 - 2 * (me % 2)
    hub = ((me + 1) // 2) % 2
    return me, near, 3 - me, hub


def greet(me):
    barrier = pltpu.get_barrier_semaphore()
    for d in range(1, N):
        pl.semaphore_signal(barrier, inc=1, device_id={"member": (me + d) % N})
    pl.semaphore_wait(barrier, N - 1)


class LineSum:
    def __init__(self, block, total, own, part, from_end, side, from_side, sems):
        self.me, self.near, self.across, self.hub = line_position()
        self.block, self.total, self.own = block, total, own
        self.part, self.from_end, self.side, self.from_side = part, from_end, side, from_side
        self.sems = sems

    def rows(self, c):
        return pl.ds(pl.multiple_of(c * self.block, self.block), self.block)

    def copy(self, kind, src, dst, layer, c, peer):
        rows = self.rows(c)
        return pltpu.make_async_remote_copy(
            src_ref=src.at[layer, rows],
            dst_ref=dst.at[layer, rows],
            send_sem=self.sems.at[2 * kind, layer, c],
            recv_sem=self.sems.at[2 * kind + 1, layer, c],
            device_id={"member": peer},
        )

    def to_hub(self, layer, c):
        return self.copy(0, self.part, self.from_end, layer, c, self.near)

    def to_side(self, layer, c):
        return self.copy(1, self.side, self.from_side, layer, c, self.across)

    def to_end(self, layer, c):
        return self.copy(2, self.total, self.total, layer, c, self.near)

    def put(self, layer, c, value):
        @pl.when(self.hub == 1)
        def _():
            self.own[self.rows(c), :] = value

        @pl.when(self.hub == 0)
        def _():
            self.part[layer, self.rows(c), :] = value.astype(BF16)

            @pl.when(c > 0)
            def _():
                self.to_hub(layer, c - 1).wait_send()

            self.to_hub(layer, c).start()

    def exchange(self, layer, c):
        rows = self.rows(c)

        @pl.when(self.hub == 1)
        def _():
            self.to_hub(layer, c).wait_recv()
            both = self.own[rows, :] + self.from_end[layer, rows, :].astype(F32)
            self.side[layer, rows, :] = both.astype(BF16)
            self.to_side(layer, c).start()

    def get(self, layer, c):
        rows = self.rows(c)

        @pl.when(self.hub == 1)
        def _():
            self.to_side(layer, c).wait_recv()
            whole = self.side[layer, rows, :].astype(F32) + self.from_side[layer, rows, :].astype(F32)
            self.total[layer, rows, :] = whole.astype(BF16)
            self.to_end(layer, c).start()

        @pl.when(self.hub == 0)
        def _():
            self.to_end(layer, c).wait_recv()

    def lag(self, hub, end):
        return hub * self.hub + end * (1 - self.hub)

    def drain(self, layer):
        @pl.when(self.hub == 1)
        def _():
            def both(c):
                self.to_side(layer, c).wait_send()
                self.to_end(layer, c).wait_send()

            each(N, both)

        @pl.when(self.hub == 0)
        def _():
            self.to_hub(layer, N - 1).wait_send()


def each(count, body):
    lax.fori_loop(0, count, lambda i, _: (body(i), 0)[1], 0)


def stage(c, body):
    @pl.when((c >= 0) & (c < N))
    def _():
        body(c)


def ranks(w_ref, k, lo, rows):
    return jnp.concatenate([w_ref[k, r, lo : lo + rows, :] for r in range(N)], axis=1)


def times_down(a, w_ref, k):
    width = w_ref.shape[2]
    halves = []
    for j in range(0, N, 2):
        right = jnp.concatenate([w_ref[k, j], w_ref[k, j + 1]], axis=1)
        halves.append(dot(a, right))
    return jnp.concatenate(halves, axis=1)


def forward_kernel(
    inv_ref, own_ref, x_ref, down_ref, up_ref, bias_ref, proj_ref,
    ordered_ref, w_ref, pw_ref, h_ref, bw_ref,
    ready, cur, own, part, from_end, side, from_side, v_out, v_own, v_in,
    sems, w_sems, v_sems,
):
    samples, width = x_ref.shape
    block = samples // N
    line = LineSum(block, h_ref, own, part, from_end, side, from_side, sems)
    me = line.me
    feats = width // E

    def send_w(k, d):
        peer = (me + d) % N
        return pltpu.make_async_remote_copy(
            src_ref=ready.at[k, peer],
            dst_ref=w_ref.at[k, me],
            send_sem=w_sems.at[0, k, peer],
            recv_sem=w_sems.at[1, k, me],
            device_id={"member": peer},
        )

    def recv_w(k, d):
        peer = (me + d) % N
        return pltpu.make_async_remote_copy(
            src_ref=ready.at[k, peer],
            dst_ref=w_ref.at[k, peer],
            send_sem=w_sems.at[0, k, peer],
            recv_sem=w_sems.at[1, k, peer],
            device_id={"member": peer},
        )

    def stage_w(k):
        source = down_ref if k % 2 == 0 else up_ref

        def one(f):
            at = pl.multiple_of((f % feats) * E, E)
            ready[k, f // feats, pl.ds(at, E), :] = source[k // 2, inv_ref[f]]

        each(N * feats, one)
        w_ref[k, me] = ready[k, me]

    def got_w(k):
        for d in range(1, N):
            recv_w(k, d).wait_recv()

    def pump(j):
        @pl.when((j > 0) & (j < 9))
        def _():
            send_w(1 + (j - 1) // 3, 1 + (j - 1) % 3).wait_send()

        @pl.when(j < 9)
        def _():
            send_w(1 + j // 3, 1 + j % 3).start()

    greet(me)
    stage_w(0)
    for d in range(1, N):
        send_w(0, d).start()
    for k in range(1, 4):
        stage_w(k)
    for i in range(feats):
        slot = inv_ref[me * feats + i]
        pw_ref[i * E : (i + 1) * E, :] = proj_ref[slot]
        for layer in range(2):
            bw_ref[layer, :, i * E : (i + 1) * E] = bias_ref[layer, slot]
    for d in range(1, N):
        send_w(0, d).wait_send()
    got_w(0)

    def first_sum(i):
        pump(i)
        stage(i, lambda c: line.put(0, c, times_down(x_ref[line.rows(c), :], w_ref, 0)))
        stage(i, lambda c: line.exchange(0, c))
        stage(i - line.lag(1, 3), lambda c: line.get(0, c))

    each(N + 3, first_sum)
    got_w(1)
    got_w(2)

    def next_current(layer, c):
        rows = line.rows(c)
        hidden = h_ref[layer, rows, :]
        for lo in range(0, width, NB):
            cols = slice(lo, lo + NB)
            scale = dot_t(hidden, ranks(w_ref, 2 * layer + 1, lo, NB)) + bw_ref[layer, :, cols]
            x = x_ref[rows, cols].astype(F32)
            before = x if layer == 0 else cur[rows, cols].astype(F32)
            cur[rows, cols] = (x * scale + before).astype(BF16)

    def v_copy(slot, peer):
        return pltpu.make_async_remote_copy(
            src_ref=v_out.at[peer],
            dst_ref=v_in.at[slot],
            send_sem=v_sems.at[0, peer],
            recv_sem=v_sems.at[1, slot],
            device_id={"member": peer},
        )

    def vectors(c):
        next_current(1, c)
        part_v = dot(cur[line.rows(c), :], pw_ref[...])

        @pl.when(c == me)
        def _():
            v_own[...] = part_v

        @pl.when(c != me)
        def _():
            v_out[c] = part_v.astype(BF16)
            v_copy(me, c).start()

    def middle(c):
        next_current(0, c)
        line.put(1, c, times_down(cur[line.rows(c), :], w_ref, 2))

    def second_sum(i):
        pump(N + 3 + i)
        stage(i, middle)
        stage(i, lambda c: line.exchange(1, c))
        stage(i - line.lag(1, 3), lambda c: line.get(1, c))

        @pl.when(i == 3)
        def _():
            got_w(3)

        stage(i - 3, vectors)

    each(N + 3, second_sum)
    vector = v_own[...]
    for d in range(1, N):
        peer = (me + d) % N
        v_copy(peer, peer).wait_recv()
        vector = vector + v_in[peer].astype(F32)
    vector = vector.astype(BF16)
    shape = (2 * block, block)
    hit = own_ref[...] == lax.broadcasted_iota(jnp.int32, shape, 1)
    odd = lax.broadcasted_iota(jnp.int32, shape, 0) % 2
    total = jnp.zeros((2 * block, E), F32)
    for k in range(2):
        pick = jnp.where(hit & (odd == k), 1.0, 0.0).astype(BF16)
        total = total + dot(pick, vector[:, k * E : (k + 1) * E])
    ordered_ref[...] = total.astype(BF16)

    send_w(3, 3).wait_send()
    for d in range(1, N):
        v_copy(me, (me + d) % N).wait_send()
    for layer in range(2):
        line.drain(layer)


def backward_kernel(
    own_ref, ret_ref, x_ref, w_ref, pw_ref, h_ref, bw_ref,
    out_ref,
    vg, grad, scales, own, part, from_end, side, from_side, dh,
    sems, v_sems,
):
    samples, width = x_ref.shape
    block = samples // N
    line = LineSum(block, dh, own, part, from_end, side, from_side, sems)
    me = line.me
    greet(me)

    shape = (block, 2 * block)
    hit = own_ref[...] == lax.broadcasted_iota(jnp.int32, shape, 0)
    odd = lax.broadcasted_iota(jnp.int32, shape, 1) % 2
    for k in range(2):
        pick = jnp.where(hit & (odd == k), 1.0, 0.0).astype(BF16)
        vg[me, :, k * E : (k + 1) * E] = dot(pick, ret_ref[...]).astype(BF16)

    def v_copy(slot, peer):
        return pltpu.make_async_remote_copy(
            src_ref=vg.at[slot],
            dst_ref=vg.at[slot],
            send_sem=v_sems.at[0, peer],
            recv_sem=v_sems.at[1, slot],
            device_id={"member": peer},
        )

    for d in range(1, N):
        v_copy(me, (me + d) % N).start()

    def scale_of(c):
        rows = line.rows(c)
        for layer in range(2):
            hidden = h_ref[layer, rows, :]
            for lo in range(0, width, NB):
                cols = slice(lo, lo + NB)
                scale = dot_t(hidden, ranks(w_ref, 2 * layer + 1, lo, NB)) + bw_ref[layer, :, cols]
                scales[layer, rows, cols] = scale

    each(N, scale_of)
    for d in range(1, N):
        v_copy((me + d) % N, (me + d) % N).wait_recv()

    def last_layer(c):
        rows = line.rows(c)
        total = jnp.zeros((block, w_ref.shape[1] * w_ref.shape[3]), F32)
        for lo in range(0, width, NB):
            cols = slice(lo, lo + NB)
            g = dot_t(vg[c], pw_ref[cols, :])
            grad[rows, cols] = g
            dscale = (g * x_ref[rows, cols].astype(F32)).astype(BF16)
            total = total + dot(dscale, ranks(w_ref, 3, lo, NB))
        line.put(0, c, total)

    def first_layer(c):
        rows = line.rows(c)
        line.get(0, c)
        dhidden = dh[0, rows, :]
        total = jnp.zeros((block, w_ref.shape[1] * w_ref.shape[3]), F32)
        for lo in range(0, width, NB):
            cols = slice(lo, lo + NB)
            g2 = grad[rows, cols]
            g1 = g2 + dot_t(dhidden, ranks(w_ref, 2, lo, NB))
            grad[rows, cols] = g1 + (g2 * scales[1, rows, cols] + g1 * scales[0, rows, cols])
            dscale = (g1 * x_ref[rows, cols].astype(F32)).astype(BF16)
            total = total + dot(dscale, ranks(w_ref, 1, lo, NB))
        line.put(1, c, total)

    def finish(c):
        rows = line.rows(c)
        line.get(1, c)
        dhidden = dh[1, rows, :]
        for lo in range(0, width, NB):
            cols = slice(lo, lo + NB)
            g0 = grad[rows, cols] + dot_t(dhidden, ranks(w_ref, 0, lo, NB))
            out_ref[rows, cols] = g0.astype(BF16)

    def both_sums(i):
        stage(i, last_layer)
        stage(i, lambda c: line.exchange(0, c))
        stage(i - line.lag(1, 3), first_layer)
        stage(i - 3, lambda c: line.exchange(1, c))
        stage(i - line.lag(4, 6), finish)

    each(N + 6, both_sums)
    for d in range(1, N):
        v_copy(me, (me + d) % N).wait_send()
    for layer in range(2):
        line.drain(layer)


def interaction_kernel(vec_ref, cot_ref, table_ref, ret_ref, got, back, sems):
    towers, packed, _ = vec_ref.shape
    owned = cot_ref.shape[0]
    vecs = cot_ref.shape[1]
    me = lax.axis_index("tower")
    barrier = pltpu.get_barrier_semaphore()

    def other(d):
        return (me + 1 + d) % towers

    each(towers - 1, lambda d: pl.semaphore_signal(barrier, inc=1, device_id={"tower": other(d)}))
    pl.semaphore_wait(barrier, towers - 1)

    def exchange(phase, src, dst):
        def copy(d):
            return pltpu.make_async_remote_copy(
                src_ref=src.at[other(d)],
                dst_ref=dst.at[me],
                send_sem=sems.at[0, phase],
                recv_sem=sems.at[1, phase],
                device_id={"tower": other(d)},
            )

        each(towers - 1, lambda d: copy(d).start())
        dst[me] = src[me]

    def arrived(which, phase, ref):
        all_but_one = ref.at[pl.ds(0, towers - 1)]
        pltpu.make_async_copy(all_but_one, all_but_one, sems.at[which, phase]).wait()

    exchange(0, vec_ref, got)
    arrived(1, 0, got)
    flat = got[...].reshape(towers * packed, E)
    shape = (vecs, towers * packed)
    row = lax.broadcasted_iota(jnp.int32, shape, 0)
    col = lax.broadcasted_iota(jnp.int32, shape, 1)
    total = jnp.zeros((towers * packed, E), F32)
    for r in range(owned):
        pick = jnp.where(col == (row // 2) * packed + 2 * r + row % 2, 1.0, 0.0).astype(BF16)
        vectors = dot(pick, flat).astype(BF16)
        table_ref[r] = dot_t(vectors, vectors) * (1.0 / E)
        cot = cot_ref[r]
        both = dot(cot, vectors) + lax.dot_general(cot, vectors, TN, preferred_element_type=F32)
        grad = (both * (1.0 / E)).astype(BF16)
        total = total + lax.dot_general(pick, grad, TN, preferred_element_type=F32)
    back[...] = total.astype(BF16).reshape(towers, packed, E)
    exchange(1, back, ret_ref)
    arrived(1, 1, ret_ref)
    for phase in range(2):
        arrived(0, phase, got)


def line_scratch(samples, rank):
    return [pltpu.VMEM((samples, rank), F32)] + [pltpu.VMEM((2, samples, rank), BF16)] * 4


def vmem():
    return pl.BlockSpec(memory_space=pltpu.VMEM)


def params(collective_id):
    return pltpu.CompilerParams(
        collective_id=collective_id, has_side_effects=True, vmem_limit_bytes=60 << 20
    )


def per_device(slabs, cross_down, cross_up, cross_bias, projector, placement, owner, inter_grad):
    x = slabs[0]
    samples, width = x.shape
    block = samples // N
    slots = placement.shape[1]
    rank = N * cross_down.shape[3]
    towers = block // 4
    order = placement[0]
    index = jnp.arange(slots, dtype=jnp.int32)
    inverse = jnp.sum(jnp.where(order[None, :] == index[:, None], index[None, :], 0), axis=1)
    own_row = lax.dynamic_index_in_dim(owner, lax.axis_index("member"), 0, keepdims=False)
    own_twice = jnp.repeat(own_row, 2)
    sds = jax.ShapeDtypeStruct
    ordered, w, pw, hidden, bw = pl.pallas_call(
        forward_kernel,
        out_shape=(
            sds((2 * block, E), BF16),
            sds((4, N, width, E), BF16),
            sds((width, 2 * E), BF16),
            sds((2, samples, rank), BF16),
            sds((2, 1, width), F32),
        ),
        in_specs=[pl.BlockSpec(memory_space=pltpu.SMEM)] + [vmem()] * 6,
        out_specs=(vmem(),) * 5,
        scratch_shapes=[
            pltpu.VMEM((4, N, width, E), BF16),
            pltpu.VMEM((samples, width), BF16),
            *line_scratch(samples, rank),
            pltpu.VMEM((N, block, 2 * E), BF16),
            pltpu.VMEM((block, 2 * E), F32),
            pltpu.VMEM((N, block, 2 * E), BF16),
            pltpu.SemaphoreType.DMA((6, 2, N)),
            pltpu.SemaphoreType.DMA((2, 4, N)),
            pltpu.SemaphoreType.DMA((2, N)),
        ],
        compiler_params=params(0),
        name="forward",
    )(
        inverse, own_twice[:, None], x,
        cross_down[0].reshape(2, slots, E, E), cross_up[0].reshape(2, slots, E, E),
        cross_bias[0].reshape(2, slots, 1, E), projector[0].reshape(slots, E, 2 * E),
    )

    table, returned = pl.pallas_call(
        interaction_kernel,
        out_shape=(sds((4, 2 * towers, 2 * towers), F32), sds((towers, 8, E), BF16)),
        in_specs=[vmem()] * 2,
        out_specs=(vmem(),) * 2,
        scratch_shapes=[pltpu.VMEM((towers, 8, E), BF16)] * 2 + [pltpu.SemaphoreType.DMA((2, 2))],
        compiler_params=params(2),
        name="interaction",
    )(ordered.reshape(towers, 8, E), inter_grad.reshape(4, 2 * towers, 2 * towers))
    interactions = table.reshape(4, -1)

    slab_grad = pl.pallas_call(
        backward_kernel,
        out_shape=sds((samples, width), BF16),
        in_specs=[vmem()] * 7,
        out_specs=vmem(),
        scratch_shapes=[
            pltpu.VMEM((N, block, 2 * E), BF16),
            pltpu.VMEM((samples, width), F32),
            pltpu.VMEM((2, samples, width), F32),
            *line_scratch(samples, rank),
            pltpu.VMEM((2, samples, rank), BF16),
            pltpu.SemaphoreType.DMA((6, 2, N)),
            pltpu.SemaphoreType.DMA((2, N)),
        ],
        compiler_params=params(1),
        name="backward",
    )(own_twice[None, :], returned.reshape(2 * block, E), x, w, pw, hidden, bw)
    return interactions, slab_grad[None]


def solution(mesh):
    placed = (
        P("tower", None, "member"),
        P("tower", None, None, "member"),
        P("tower", None, None, "member"),
        P("tower", None, None),
        P("tower", None, None),
        P("tower", None),
        P(),
        P(("tower", "member"), None),
    )
    return jax.shard_map(
        per_device,
        mesh=mesh,
        in_specs=placed,
        out_specs=(P(("tower", "member"), None), P("tower", None, "member")),
        check_vma=False,
    )
```

```python
import jax
import jax.numpy as jnp
from jax import lax
from jax.experimental import pallas as pl
from jax.experimental.pallas import tpu as pltpu
from jax.sharding import PartitionSpec as P

F32 = jnp.float32
BF16 = jnp.bfloat16
E = 128
N = 4
PUMPS = ((1, 0), (2, 2), (3, 5))
NB = 256
NT = (((1,), (1,)), ((), ()))
TN = (((0,), (0,)), ((), ()))


def dot(a, b):
    return jnp.dot(a, b, preferred_element_type=F32)


def dot_t(a, b):
    return lax.dot_general(a, b, NT, preferred_element_type=F32)


def line_position():
    me = lax.axis_index("member")
    near = me + 1 - 2 * (me % 2)
    hub = ((me + 1) // 2) % 2
    return me, near, 3 - me, hub


class LineSum:
    def __init__(self, block, total, own, mine, from_end, from_side, sems):
        self.me, self.near, self.across, self.hub = line_position()
        self.block, self.total, self.own = block, total, own
        self.mine, self.from_end, self.from_side = mine, from_end, from_side
        self.sems = sems

    def rows(self, c):
        return pl.ds(pl.multiple_of(c * self.block, self.block), self.block)

    def copy(self, kind, src, dst, n, c, peer):
        rows = self.rows(c)
        return pltpu.make_async_remote_copy(
            src_ref=src.at[n, rows],
            dst_ref=dst.at[n, rows],
            send_sem=self.sems.at[2 * kind, n, c],
            recv_sem=self.sems.at[2 * kind + 1, n, c],
            device_id={"member": peer},
        )

    def to_hub(self, n, c):
        return self.copy(0, self.mine, self.from_end, n, c, self.near)

    def to_side(self, n, c):
        return self.copy(1, self.mine, self.from_side, n, c, self.across)

    def to_end(self, n, c):
        return self.copy(2, self.total, self.total, n, c, self.near)

    def put(self, n, c, value):
        @pl.when(self.hub == 1)
        def _():
            self.own[self.rows(c), :] = value

        @pl.when(self.hub == 0)
        def _():
            self.mine[n, self.rows(c), :] = value.astype(BF16)

            @pl.when(c > 0)
            def _():
                self.to_hub(n, c - 1).wait_send()

            self.to_hub(n, c).start()

    def exchange(self, n, c):
        rows = self.rows(c)

        @pl.when(self.hub == 1)
        def _():
            self.to_hub(n, c).wait_recv()
            both = self.own[rows, :] + self.from_end[n, rows, :].astype(F32)
            self.mine[n, rows, :] = both.astype(BF16)
            self.to_side(n, c).start()

    def get(self, n, c):
        rows = self.rows(c)

        @pl.when(self.hub == 1)
        def _():
            self.to_side(n, c).wait_recv()
            whole = self.mine[n, rows, :].astype(F32) + self.from_side[n, rows, :].astype(F32)
            self.total[n, rows, :] = whole.astype(BF16)
            self.to_end(n, c).start()

        @pl.when(self.hub == 0)
        def _():
            self.to_end(n, c).wait_recv()

    def lag(self, hub, end):
        return hub * self.hub + end * (1 - self.hub)

    def drain(self, n):
        @pl.when(self.hub == 1)
        def _():
            def both(c):
                self.to_side(n, c).wait_send()
                self.to_end(n, c).wait_send()

            each(N, both)

        @pl.when(self.hub == 0)
        def _():
            self.to_hub(n, N - 1).wait_send()


def each(count, body):
    lax.fori_loop(0, count, lambda i, _: (body(i), 0)[1], 0)


def stage(c, body):
    @pl.when((c >= 0) & (c < N))
    def _():
        body(c)


def ranks(w_ref, k, lo, rows):
    return jnp.concatenate([w_ref[k, r, lo : lo + rows, :] for r in range(N)], axis=1)


def times_down(a, w_ref, k):
    width = w_ref.shape[2]
    halves = []
    for j in range(0, N, 2):
        right = jnp.concatenate([w_ref[k, j], w_ref[k, j + 1]], axis=1)
        halves.append(dot(a, right))
    return jnp.concatenate(halves, axis=1)


def step_kernel(
    inv_ref, own_col_ref, own_row_ref, x_hbm, down_hbm, up_hbm, bias_ref, proj_hbm, cot_ref,
    out_ref, table_ref,
    x_ref, map0, map1, map2, map3, proj_ref, ready, w_ref, pw_ref, bw_ref, cur, scales, grad,
    own, total_ref, mine, from_end, from_side, v_out, v_own, v_in, vg, ordered, got, back, ret,
    load_sems, sems, w_sems, v_sems, g_sems, t_sems,
):
    samples, width = x_ref.shape
    block = samples // N
    rank = N * E
    feats = width // E
    towers, packed, _ = ordered.shape
    owned, vecs = cot_ref.shape[:2]
    line = LineSum(block, total_ref, own, mine, from_end, from_side, sems)
    me = line.me
    tower = lax.axis_index("tower")

    def other(d):
        return (tower + 1 + d) % towers

    loads = [
        pltpu.make_async_copy(src, dst, load_sems.at[i])
        for i, (src, dst) in enumerate(
            (
                (down_hbm.at[0], map0),
                (x_hbm, x_ref),
                (up_hbm.at[0], map1),
                (down_hbm.at[1], map2),
                (up_hbm.at[1], map3),
                (proj_hbm, proj_ref),
            )
        )
    ]
    for load in loads:
        load.start()
    barrier = pltpu.get_barrier_semaphore()
    for d in range(1, N):
        pl.semaphore_signal(barrier, inc=1, device_id={"member": (me + d) % N})
    each(towers - 1, lambda d: pl.semaphore_signal(barrier, inc=1, device_id={"tower": other(d)}))

    def send_w(k, d):
        peer = (me + d) % N
        return pltpu.make_async_remote_copy(
            src_ref=ready.at[k, peer],
            dst_ref=w_ref.at[k, me],
            send_sem=w_sems.at[0, k, peer],
            recv_sem=w_sems.at[1, k, me],
            device_id={"member": peer},
        )

    def recv_w(k, d):
        peer = (me + d) % N
        return pltpu.make_async_remote_copy(
            src_ref=ready.at[k, peer],
            dst_ref=w_ref.at[k, peer],
            send_sem=w_sems.at[0, k, peer],
            recv_sem=w_sems.at[1, k, peer],
            device_id={"member": peer},
        )

    def make_ready(k):
        source = (map0, map1, map2, map3)[k]

        def one(f):
            at = pl.multiple_of((f % feats) * E, E)
            ready[k, f // feats, pl.ds(at, E), :] = source[inv_ref[f]]

        each(N * feats, one)
        w_ref[k, me] = ready[k, me]

    def start_w(k):
        for d in range(1, N):
            send_w(k, d).start()

    def sent_w(k):
        for d in range(1, N):
            send_w(k, d).wait_send()

    def got_w(k):
        for d in range(1, N):
            recv_w(k, d).wait_recv()

    def pump(i):
        for k, at in PUMPS:

            @pl.when(i == at)
            def _():
                if k > 1:
                    sent_w(k - 1)
                start_w(k)

    loads[0].wait()
    make_ready(0)
    pl.semaphore_wait(barrier, N - 1 + towers - 1)
    start_w(0)
    for load in loads[1:]:
        load.wait()
    for k in range(1, 4):
        make_ready(k)
    for i in range(feats):
        slot = inv_ref[me * feats + i]
        pw_ref[i * E : (i + 1) * E, :] = proj_ref[slot]
        for layer in range(2):
            bw_ref[layer, :, i * E : (i + 1) * E] = bias_ref[layer, slot]
    sent_w(0)
    got_w(0)

    def first_sum(i):
        pump(i)
        stage(i, lambda c: line.put(0, c, times_down(x_ref[line.rows(c), :], w_ref, 0)))
        stage(i, lambda c: line.exchange(0, c))
        stage(i - line.lag(1, 3), lambda c: line.get(0, c))

    each(N + 3, first_sum)
    got_w(1)
    got_w(2)

    def next_current(layer, c):
        rows = line.rows(c)
        hidden = total_ref[layer, rows, :]
        for lo in range(0, width, NB):
            cols = slice(lo, lo + NB)
            scale = dot_t(hidden, ranks(w_ref, 2 * layer + 1, lo, NB)) + bw_ref[layer, :, cols]
            scales[layer, rows, cols] = scale
            x = x_ref[rows, cols].astype(F32)
            before = x if layer == 0 else cur[rows, cols].astype(F32)
            cur[rows, cols] = (x * scale + before).astype(BF16)

    def v_copy(slot, peer):
        return pltpu.make_async_remote_copy(
            src_ref=v_out.at[peer],
            dst_ref=v_in.at[slot],
            send_sem=v_sems.at[0, peer],
            recv_sem=v_sems.at[1, slot],
            device_id={"member": peer},
        )

    def vectors(c):
        next_current(1, c)
        part_v = dot(cur[line.rows(c), :], pw_ref[...])

        @pl.when(c == me)
        def _():
            v_own[...] = part_v

        @pl.when(c != me)
        def _():
            v_out[c] = part_v.astype(BF16)
            v_copy(me, c).start()

    def middle(c):
        next_current(0, c)
        line.put(1, c, times_down(cur[line.rows(c), :], w_ref, 2))

    def second_sum(i):
        pump(N + 3 + i)
        stage(i, middle)
        stage(i, lambda c: line.exchange(1, c))
        stage(i - line.lag(1, 3), lambda c: line.get(1, c))

        @pl.when(i == 3)
        def _():
            got_w(3)

        stage(i - 3, vectors)

    each(N + 3, second_sum)
    vector = v_own[...]
    for d in range(1, N):
        peer = (me + d) % N
        v_copy(peer, peer).wait_recv()
        vector = vector + v_in[peer].astype(F32)
    vector = vector.astype(BF16)
    shape = (2 * block, block)
    hit = own_col_ref[...] == lax.broadcasted_iota(jnp.int32, shape, 1)
    odd = lax.broadcasted_iota(jnp.int32, shape, 0) % 2
    total = jnp.zeros((2 * block, E), F32)
    for k in range(2):
        pick = jnp.where(hit & (odd == k), 1.0, 0.0).astype(BF16)
        total = total + dot(pick, vector[:, k * E : (k + 1) * E])
    ordered[...] = total.astype(BF16).reshape(towers, packed, E)

    def swap(phase, src, dst):
        def copy(d):
            return pltpu.make_async_remote_copy(
                src_ref=src.at[other(d)],
                dst_ref=dst.at[tower],
                send_sem=t_sems.at[0, phase],
                recv_sem=t_sems.at[1, phase],
                device_id={"tower": other(d)},
            )

        each(towers - 1, lambda d: copy(d).start())
        dst[tower] = src[tower]

    def arrived(which, phase, ref):
        all_but_one = ref.at[pl.ds(0, towers - 1)]
        pltpu.make_async_copy(all_but_one, all_but_one, t_sems.at[which, phase]).wait()

    swap(0, ordered, got)
    shape = (vecs, towers * packed)
    row = lax.broadcasted_iota(jnp.int32, shape, 0)
    col = lax.broadcasted_iota(jnp.int32, shape, 1)
    arrived(1, 0, got)
    flat = got[...].reshape(towers * packed, E)
    total = jnp.zeros((towers * packed, E), F32)
    held = []
    for r in range(owned):
        pick = jnp.where(col == (row // 2) * packed + 2 * r + row % 2, 1.0, 0.0).astype(BF16)
        vecs_r = dot(pick, flat).astype(BF16)
        held.append(vecs_r)
        cot = cot_ref[r]
        both = dot(cot, vecs_r) + lax.dot_general(cot, vecs_r, TN, preferred_element_type=F32)
        g = (both * (1.0 / E)).astype(BF16)
        total = total + lax.dot_general(pick, g, TN, preferred_element_type=F32)
    back[...] = total.astype(BF16).reshape(towers, packed, E)
    swap(1, back, ret)
    for r in range(owned):
        table_ref[r] = dot_t(held[r], held[r]) * (1.0 / E)
    arrived(1, 1, ret)

    shape = (block, 2 * block)
    hit = own_row_ref[...] == lax.broadcasted_iota(jnp.int32, shape, 0)
    odd = lax.broadcasted_iota(jnp.int32, shape, 1) % 2
    flat = ret[...].reshape(towers * packed, E)
    for k in range(2):
        pick = jnp.where(hit & (odd == k), 1.0, 0.0).astype(BF16)
        vg[me, :, k * E : (k + 1) * E] = dot(pick, flat).astype(BF16)

    def g_copy(slot, peer):
        return pltpu.make_async_remote_copy(
            src_ref=vg.at[slot],
            dst_ref=vg.at[slot],
            send_sem=g_sems.at[0, peer],
            recv_sem=g_sems.at[1, slot],
            device_id={"member": peer},
        )

    for d in range(1, N):
        g_copy(me, (me + d) % N).start()

    def last_layer(c):
        rows = line.rows(c)

        @pl.when(c != me)
        def _():
            g_copy(c, c).wait_recv()

        total = jnp.zeros((block, rank), F32)
        for lo in range(0, width, NB):
            cols = slice(lo, lo + NB)
            g = dot_t(vg[c], pw_ref[cols, :])
            grad[rows, cols] = g
            dscale = (g * x_ref[rows, cols].astype(F32)).astype(BF16)
            total = total + dot(dscale, ranks(w_ref, 3, lo, NB))
        line.put(2, c, total)

    def first_layer(c):
        rows = line.rows(c)
        line.get(2, c)
        dhidden = total_ref[2, rows, :]
        total = jnp.zeros((block, rank), F32)
        for lo in range(0, width, NB):
            cols = slice(lo, lo + NB)
            g2 = grad[rows, cols]
            g1 = g2 + dot_t(dhidden, ranks(w_ref, 2, lo, NB))
            grad[rows, cols] = g1 + (g2 * scales[1, rows, cols] + g1 * scales[0, rows, cols])
            dscale = (g1 * x_ref[rows, cols].astype(F32)).astype(BF16)
            total = total + dot(dscale, ranks(w_ref, 1, lo, NB))
        line.put(3, c, total)

    def finish(c):
        rows = line.rows(c)
        line.get(3, c)
        dhidden = total_ref[3, rows, :]
        for lo in range(0, width, NB):
            cols = slice(lo, lo + NB)
            g0 = grad[rows, cols] + dot_t(dhidden, ranks(w_ref, 0, lo, NB))
            out_ref[rows, cols] = g0.astype(BF16)

    def both_sums(i):
        stage(i, last_layer)
        stage(i, lambda c: line.exchange(2, c))
        stage(i - line.lag(1, 3), first_layer)
        stage(i - 3, lambda c: line.exchange(3, c))
        stage(i - line.lag(4, 6), finish)

    each(N + 6, both_sums)

    sent_w(3)
    for d in range(1, N):
        v_copy(me, (me + d) % N).wait_send()
        g_copy(me, (me + d) % N).wait_send()
    for phase in range(2):
        arrived(0, phase, got)
    for n in range(4):
        line.drain(n)


def vmem():
    return pl.BlockSpec(memory_space=pltpu.VMEM)


def params(collective_id):
    return pltpu.CompilerParams(
        collective_id=collective_id, has_side_effects=True, vmem_limit_bytes=62 << 20
    )


def per_device(slabs, cross_down, cross_up, cross_bias, projector, placement, owner, inter_grad):
    x = slabs[0]
    samples, width = x.shape
    block = samples // N
    slots = placement.shape[1]
    rank = N * cross_down.shape[3]
    towers = block // 4
    order = placement[0]
    index = jnp.arange(slots, dtype=jnp.int32)
    inverse = jnp.sum(jnp.where(order[None, :] == index[:, None], index[None, :], 0), axis=1)
    own_row = lax.dynamic_index_in_dim(owner, lax.axis_index("member"), 0, keepdims=False)
    own_twice = jnp.repeat(own_row, 2)
    sds = jax.ShapeDtypeStruct
    dma = pltpu.SemaphoreType.DMA
    any_spec = pl.BlockSpec(memory_space=pl.ANY)
    slab_grad, table = pl.pallas_call(
        step_kernel,
        out_shape=(sds((samples, width), BF16), sds((4, 2 * towers, 2 * towers), F32)),
        in_specs=[
            pl.BlockSpec(memory_space=pltpu.SMEM), vmem(), vmem(), any_spec, any_spec, any_spec,
            vmem(), any_spec, vmem(),
        ],
        out_specs=(vmem(),) * 2,
        scratch_shapes=[
            pltpu.VMEM((samples, width), BF16),
            *[pltpu.VMEM((slots, E, E), BF16)] * 4,
            pltpu.VMEM((slots, E, 2 * E), BF16),
            pltpu.VMEM((4, N, width, E), BF16),
            pltpu.VMEM((4, N, width, E), BF16),
            pltpu.VMEM((width, 2 * E), BF16),
            pltpu.VMEM((2, 1, width), F32),
            pltpu.VMEM((samples, width), BF16),
            pltpu.VMEM((2, samples, width), F32),
            pltpu.VMEM((samples, width), F32),
            pltpu.VMEM((samples, rank), F32),
            *[pltpu.VMEM((4, samples, rank), BF16)] * 4,
            pltpu.VMEM((N, block, 2 * E), BF16),
            pltpu.VMEM((block, 2 * E), F32),
            pltpu.VMEM((N, block, 2 * E), BF16),
            pltpu.VMEM((N, block, 2 * E), BF16),
            *[pltpu.VMEM((towers, 8, E), BF16)] * 4,
            dma((6,)),
            dma((6, 4, N)),
            dma((2, 4, N)),
            dma((2, N)),
            dma((2, N)),
            dma((2, 2)),
        ],
        compiler_params=params(0),
        name="mega",
    )(
        inverse, own_twice[:, None], own_twice[None, :], x,
        cross_down[0].reshape(2, slots, E, E), cross_up[0].reshape(2, slots, E, E),
        cross_bias[0].reshape(2, slots, 1, E), projector[0].reshape(slots, E, 2 * E),
        inter_grad.reshape(4, 2 * towers, 2 * towers),
    )
    interactions = table.reshape(4, -1)
    return interactions, slab_grad[None]


def solution(mesh):
    placed = (
        P("tower", None, "member"),
        P("tower", None, None, "member"),
        P("tower", None, None, "member"),
        P("tower", None, None),
        P("tower", None, None),
        P("tower", None),
        P(),
        P(("tower", "member"), None),
    )
    return jax.shard_map(
        per_device,
        mesh=mesh,
        in_specs=placed,
        out_specs=(P(("tower", "member"), None), P("tower", None, "member")),
        check_vma=False,
    )
```

```python
import jax
import jax.numpy as jnp
from jax import lax
from jax.experimental import pallas as pl
from jax.experimental.pallas import tpu as pltpu
from jax.sharding import PartitionSpec as P

F32 = jnp.float32
BF16 = jnp.bfloat16
E = 128
N = 4
PUMPS = ((1, 0), (2, 4), (3, 7))
NB = 256
NT = (((1,), (1,)), ((), ()))
TN = (((0,), (0,)), ((), ()))


def dot(a, b):
    return jnp.dot(a, b, preferred_element_type=F32)


def dot_t(a, b):
    return lax.dot_general(a, b, NT, preferred_element_type=F32)


def line_position():
    me = lax.axis_index("member")
    near = me + 1 - 2 * (me % 2)
    hub = ((me + 1) // 2) % 2
    return me, near, 3 - me, hub


class LineSum:
    def __init__(self, block, total, own, mine, from_end, from_side, sems):
        self.me, self.near, self.across, self.hub = line_position()
        self.block, self.total, self.own = block, total, own
        self.mine, self.from_end, self.from_side = mine, from_end, from_side
        self.sems = sems

    def rows(self, c):
        return pl.ds(pl.multiple_of(c * self.block, self.block), self.block)

    def copy(self, kind, src, dst, n, c, peer):
        rows = self.rows(c)
        return pltpu.make_async_remote_copy(
            src_ref=src.at[n, rows],
            dst_ref=dst.at[n, rows],
            send_sem=self.sems.at[2 * kind, n, c],
            recv_sem=self.sems.at[2 * kind + 1, n, c],
            device_id={"member": peer},
        )

    def to_hub(self, n, c):
        return self.copy(0, self.mine, self.from_end, n, c, self.near)

    def to_side(self, n, c):
        return self.copy(1, self.mine, self.from_side, n, c, self.across)

    def to_end(self, n, c):
        return self.copy(2, self.total, self.total, n, c, self.near)

    def put(self, n, c, value):
        @pl.when(self.hub == 1)
        def _():
            self.own[self.rows(c), :] = value

        @pl.when(self.hub == 0)
        def _():
            self.mine[n, self.rows(c), :] = value.astype(BF16)

            @pl.when(c > 0)
            def _():
                self.to_hub(n, c - 1).wait_send()

            self.to_hub(n, c).start()

    def exchange(self, n, c):
        rows = self.rows(c)

        @pl.when(self.hub == 1)
        def _():
            self.to_hub(n, c).wait_recv()
            both = self.own[rows, :] + self.from_end[n, rows, :].astype(F32)
            self.mine[n, rows, :] = both.astype(BF16)
            self.to_side(n, c).start()

    def get(self, n, c):
        rows = self.rows(c)

        @pl.when(self.hub == 1)
        def _():
            self.to_side(n, c).wait_recv()
            whole = self.mine[n, rows, :].astype(F32) + self.from_side[n, rows, :].astype(F32)
            self.total[n, rows, :] = whole.astype(BF16)
            self.to_end(n, c).start()

        @pl.when(self.hub == 0)
        def _():
            self.to_end(n, c).wait_recv()

    def lag(self, hub, end):
        return hub * self.hub + end * (1 - self.hub)

    def drain(self, n):
        @pl.when(self.hub == 1)
        def _():
            def both(c):
                self.to_side(n, c).wait_send()
                self.to_end(n, c).wait_send()

            each(N, both)

        @pl.when(self.hub == 0)
        def _():
            self.to_hub(n, N - 1).wait_send()


def each(count, body):
    lax.fori_loop(0, count, lambda i, _: (body(i), 0)[1], 0)


def stage(c, body):
    @pl.when((c >= 0) & (c < N))
    def _():
        body(c)


def ranks(w_ref, k, lo, rows):
    return jnp.concatenate([w_ref[k, r, lo : lo + rows, :] for r in range(N)], axis=1)


def times_down(a, w_ref, k):
    width = w_ref.shape[2]
    halves = []
    for j in range(0, N, 2):
        right = jnp.concatenate([w_ref[k, j], w_ref[k, j + 1]], axis=1)
        halves.append(dot(a, right))
    return jnp.concatenate(halves, axis=1)


def step_kernel(
    inv_ref, owner_ref, x_hbm, down_hbm, up_hbm, bias_ref, proj_hbm, cot_ref,
    out_ref, inter_ref,
    x_ref, map0, map1, map2, map3, proj_ref, ready, w_ref, pw_ref, bw_ref, cur, scales, grad,
    own, total_ref, mine, from_end, from_side, v_out, v_own, v_in, vg, ordered, got, back, ret,
    bias_slots, picks, cots, tables,
    load_sems, sems, w_sems, v_sems, g_sems, t_sems,
):
    samples, width = x_ref.shape
    block = samples // N
    rank = N * E
    feats = width // E
    towers, packed, _ = ordered.shape
    vecs, owned, _ = cots.shape
    line = LineSum(block, total_ref, own, mine, from_end, from_side, sems)
    me = line.me
    tower = lax.axis_index("tower")

    def other(d):
        return (tower + 1 + d) % towers

    loads = [
        pltpu.make_async_copy(src, dst, load_sems.at[i])
        for i, (src, dst) in enumerate(
            (
                (down_hbm.at[0], map0),
                (x_hbm, x_ref),
                (up_hbm.at[0], map1),
                (down_hbm.at[1], map2),
                (up_hbm.at[1], map3),
                (proj_hbm, proj_ref),
            )
        )
    ]
    for load in loads:
        load.start()
    barrier = pltpu.get_barrier_semaphore()
    for d in range(1, N):
        pl.semaphore_signal(barrier, inc=1, device_id={"member": (me + d) % N})
    each(towers - 1, lambda d: pl.semaphore_signal(barrier, inc=1, device_id={"tower": other(d)}))

    def send_w(k, d):
        peer = (me + d) % N
        return pltpu.make_async_remote_copy(
            src_ref=ready.at[k, peer],
            dst_ref=w_ref.at[k, me],
            send_sem=w_sems.at[0, k, peer],
            recv_sem=w_sems.at[1, k, me],
            device_id={"member": peer},
        )

    def recv_w(k, d):
        peer = (me + d) % N
        return pltpu.make_async_remote_copy(
            src_ref=ready.at[k, peer],
            dst_ref=w_ref.at[k, peer],
            send_sem=w_sems.at[0, k, peer],
            recv_sem=w_sems.at[1, k, peer],
            device_id={"member": peer},
        )

    def make_ready(k):
        source = (map0, map1, map2, map3)[k]

        def one(f):
            at = pl.multiple_of((f % feats) * E, E)
            ready[k, f // feats, pl.ds(at, E), :] = source[inv_ref[f]]

        each(N * feats, one)
        w_ref[k, me] = ready[k, me]

    def start_w(k):
        for d in range(1, N):
            send_w(k, d).start()

    def sent_w(k):
        for d in range(1, N):
            send_w(k, d).wait_send()

    def got_w(k):
        for d in range(1, N):
            recv_w(k, d).wait_recv()

    def pump(i):
        for k, at in PUMPS:

            @pl.when(i == at)
            def _():
                if k > 1:
                    sent_w(k - 1)
                start_w(k)

    loads[0].wait()
    make_ready(0)
    pl.semaphore_wait(barrier, N - 1 + towers - 1)
    start_w(0)
    for load in loads[1:]:
        load.wait()
    for k in range(1, 4):
        make_ready(k)
    for j in range(N * feats):
        bias_slots[j] = bias_ref[:, j * E : (j + 1) * E]
    for i in range(feats):
        slot = inv_ref[me * feats + i]
        pw_ref[i * E : (i + 1) * E, :] = proj_ref[slot]
        bias = bias_slots[slot]
        for layer in range(2):
            bw_ref[layer, :, i * E : (i + 1) * E] = bias[layer : layer + 1]
    places = lax.broadcasted_iota(jnp.int32, (block, block), 0)
    owns = jnp.where(owner_ref[pl.ds(me, 1), :] == places, 1.0, 0.0).astype(BF16)
    shape = (2 * block, block)
    row = lax.broadcasted_iota(jnp.int32, shape, 0)
    col = lax.broadcasted_iota(jnp.int32, shape, 1)
    for k in range(2):
        spread = jnp.where(row == 2 * col + k, 1.0, 0.0).astype(BF16)
        picks[k] = dot_t(spread, owns).astype(BF16)
    for i in range(vecs):
        cots[i] = cot_ref[:, i * E : (i + 1) * E].astype(F32)
    sent_w(0)
    got_w(0)

    def first_sum(i):
        pump(i)
        stage(i, lambda c: line.put(0, c, times_down(x_ref[line.rows(c), :], w_ref, 0)))
        stage(i, lambda c: line.exchange(0, c))
        stage(i - line.lag(1, 3), lambda c: line.get(0, c))

    each(N + 3, first_sum)
    got_w(1)
    got_w(2)

    def next_current(layer, c):
        rows = line.rows(c)
        hidden = total_ref[layer, rows, :]
        for lo in range(0, width, NB):
            cols = slice(lo, lo + NB)
            scale = dot_t(hidden, ranks(w_ref, 2 * layer + 1, lo, NB)) + bw_ref[layer, :, cols]
            scales[layer, rows, cols] = scale
            x = x_ref[rows, cols].astype(F32)
            before = x if layer == 0 else cur[rows, cols].astype(F32)
            cur[rows, cols] = (x * scale + before).astype(BF16)

    def v_copy(slot, peer):
        return pltpu.make_async_remote_copy(
            src_ref=v_out.at[peer],
            dst_ref=v_in.at[slot],
            send_sem=v_sems.at[0, peer],
            recv_sem=v_sems.at[1, slot],
            device_id={"member": peer},
        )

    def vectors(c):
        next_current(1, c)
        part_v = dot(cur[line.rows(c), :], pw_ref[...])

        @pl.when(c == me)
        def _():
            v_own[...] = part_v

        @pl.when(c != me)
        def _():
            v_out[c] = part_v.astype(BF16)
            v_copy(me, c).start()

    def middle(c):
        next_current(0, c)
        line.put(1, c, times_down(cur[line.rows(c), :], w_ref, 2))

    def second_sum(i):
        pump(N + 3 + i)
        stage(i, middle)
        stage(i, lambda c: line.exchange(1, c))
        stage(i - line.lag(1, 3), lambda c: line.get(1, c))

        @pl.when(i == 3)
        def _():
            got_w(3)

        stage(i - 3, vectors)

    each(N + 3, second_sum)
    vector = v_own[...]
    for d in range(1, N):
        peer = (me + d) % N
        v_copy(peer, peer).wait_recv()
        vector = vector + v_in[peer].astype(F32)
    vector = vector.astype(BF16)
    total = jnp.zeros((2 * block, E), F32)
    for k in range(2):
        total = total + dot(picks[k], vector[:, k * E : (k + 1) * E])
    ordered[...] = total.astype(BF16).reshape(towers, packed, E)

    def swap(phase, src, dst):
        def copy(d):
            return pltpu.make_async_remote_copy(
                src_ref=src.at[other(d)],
                dst_ref=dst.at[tower],
                send_sem=t_sems.at[0, phase],
                recv_sem=t_sems.at[1, phase],
                device_id={"tower": other(d)},
            )

        each(towers - 1, lambda d: copy(d).start())
        dst[tower] = src[tower]

    def arrived(which, phase, ref):
        all_but_one = ref.at[pl.ds(0, towers - 1)]
        pltpu.make_async_copy(all_but_one, all_but_one, t_sems.at[which, phase]).wait()

    swap(0, ordered, got)
    shape = (vecs, towers * packed)
    row = lax.broadcasted_iota(jnp.int32, shape, 0)
    col = lax.broadcasted_iota(jnp.int32, shape, 1)
    arrived(1, 0, got)
    flat = got[...].reshape(towers * packed, E)
    total = jnp.zeros((towers * packed, E), F32)
    held = []
    for r in range(owned):
        pick = jnp.where(col == (row // 2) * packed + 2 * r + row % 2, 1.0, 0.0).astype(BF16)
        vecs_r = dot(pick, flat).astype(BF16)
        held.append(vecs_r)
        cot = cots[:, r, :].astype(BF16)
        both = dot(cot, vecs_r) + lax.dot_general(cot, vecs_r, TN, preferred_element_type=F32)
        g = (both * (1.0 / E)).astype(BF16)
        total = total + lax.dot_general(pick, g, TN, preferred_element_type=F32)
    back[...] = total.astype(BF16).reshape(towers, packed, E)
    swap(1, back, ret)
    for r in range(owned):
        tables[:, r, :] = dot_t(held[r], held[r]) * (1.0 / E)
    for i in range(vecs):
        inter_ref[:, i * E : (i + 1) * E] = tables[i]
    arrived(1, 1, ret)

    flat = ret[...].reshape(towers * packed, E)
    for k in range(2):
        vg[me, :, k * E : (k + 1) * E] = lax.dot_general(
            picks[k], flat, TN, preferred_element_type=F32
        ).astype(BF16)

    def g_copy(slot, peer):
        return pltpu.make_async_remote_copy(
            src_ref=vg.at[slot],
            dst_ref=vg.at[slot],
            send_sem=g_sems.at[0, peer],
            recv_sem=g_sems.at[1, slot],
            device_id={"member": peer},
        )

    for d in range(1, N):
        g_copy(me, (me + d) % N).start()

    def last_layer(c):
        rows = line.rows(c)

        @pl.when(c != me)
        def _():
            g_copy(c, c).wait_recv()

        total = jnp.zeros((block, rank), F32)
        for lo in range(0, width, NB):
            cols = slice(lo, lo + NB)
            g = dot_t(vg[c], pw_ref[cols, :])
            grad[rows, cols] = g
            dscale = (g * x_ref[rows, cols].astype(F32)).astype(BF16)
            total = total + dot(dscale, ranks(w_ref, 3, lo, NB))
        line.put(2, c, total)

    def first_layer(c):
        rows = line.rows(c)
        line.get(2, c)
        dhidden = total_ref[2, rows, :]
        total = jnp.zeros((block, rank), F32)
        for lo in range(0, width, NB):
            cols = slice(lo, lo + NB)
            g2 = grad[rows, cols]
            g1 = g2 + dot_t(dhidden, ranks(w_ref, 2, lo, NB))
            grad[rows, cols] = g1 + (g2 * scales[1, rows, cols] + g1 * scales[0, rows, cols])
            dscale = (g1 * x_ref[rows, cols].astype(F32)).astype(BF16)
            total = total + dot(dscale, ranks(w_ref, 1, lo, NB))
        line.put(3, c, total)

    def finish(c):
        rows = line.rows(c)
        line.get(3, c)
        dhidden = total_ref[3, rows, :]
        for lo in range(0, width, NB):
            cols = slice(lo, lo + NB)
            g0 = grad[rows, cols] + dot_t(dhidden, ranks(w_ref, 0, lo, NB))
            out_ref[rows, cols] = g0.astype(BF16)

    def both_sums(i):
        stage(i, last_layer)
        stage(i, lambda c: line.exchange(2, c))
        stage(i - line.lag(1, 3), first_layer)
        stage(i - 3, lambda c: line.exchange(3, c))
        stage(i - line.lag(4, 6), finish)

    each(N + 6, both_sums)

    sent_w(3)
    for d in range(1, N):
        v_copy(me, (me + d) % N).wait_send()
        g_copy(me, (me + d) % N).wait_send()
    for phase in range(2):
        arrived(0, phase, got)
    for n in range(4):
        line.drain(n)


def vmem():
    return pl.BlockSpec(memory_space=pltpu.VMEM)


def params(collective_id):
    return pltpu.CompilerParams(
        collective_id=collective_id, has_side_effects=True, vmem_limit_bytes=62 << 20
    )


def per_device(slabs, cross_down, cross_up, cross_bias, projector, placement, owner, inter_grad):
    x = slabs[0]
    samples, width = x.shape
    block = samples // N
    slots = placement.shape[1]
    rank = N * cross_down.shape[3]
    towers = block // 4
    order = placement[0]
    index = jnp.arange(slots, dtype=jnp.int32)
    inverse = jnp.sum(jnp.where(order[None, :] == index[:, None], index[None, :], 0), axis=1)
    sds = jax.ShapeDtypeStruct
    dma = pltpu.SemaphoreType.DMA
    any_spec = pl.BlockSpec(memory_space=pl.ANY)
    slab_grad, interactions = pl.pallas_call(
        step_kernel,
        out_shape=(sds((samples, width), BF16), sds(inter_grad.shape, F32)),
        in_specs=[
            pl.BlockSpec(memory_space=pltpu.SMEM), vmem(), any_spec, any_spec, any_spec,
            vmem(), any_spec, vmem(),
        ],
        out_specs=(vmem(),) * 2,
        scratch_shapes=[
            pltpu.VMEM((samples, width), BF16),
            *[pltpu.VMEM((slots, E, E), BF16)] * 4,
            pltpu.VMEM((slots, E, 2 * E), BF16),
            pltpu.VMEM((4, N, width, E), BF16),
            pltpu.VMEM((4, N, width, E), BF16),
            pltpu.VMEM((width, 2 * E), BF16),
            pltpu.VMEM((2, 1, width), F32),
            pltpu.VMEM((samples, width), BF16),
            pltpu.VMEM((2, samples, width), F32),
            pltpu.VMEM((samples, width), F32),
            pltpu.VMEM((samples, rank), F32),
            *[pltpu.VMEM((4, samples, rank), BF16)] * 4,
            pltpu.VMEM((N, block, 2 * E), BF16),
            pltpu.VMEM((block, 2 * E), F32),
            pltpu.VMEM((N, block, 2 * E), BF16),
            pltpu.VMEM((N, block, 2 * E), BF16),
            *[pltpu.VMEM((towers, 8, E), BF16)] * 4,
            pltpu.VMEM((slots, 2, E), F32),
            pltpu.VMEM((2, 2 * block, block), BF16),
            *[pltpu.VMEM((2 * towers, inter_grad.shape[0], E), F32)] * 2,
            dma((6,)),
            dma((6, 4, N)),
            dma((2, 4, N)),
            dma((2, N)),
            dma((2, N)),
            dma((2, 2)),
        ],
        compiler_params=params(0),
        name="mega",
    )(
        inverse, owner, x,
        cross_down[0].reshape(2, slots, E, E), cross_up[0].reshape(2, slots, E, E),
        cross_bias[0], projector[0].reshape(slots, E, 2 * E), inter_grad,
    )
    return interactions, slab_grad[None]


def solution(mesh):
    placed = (
        P("tower", None, "member"),
        P("tower", None, None, "member"),
        P("tower", None, None, "member"),
        P("tower", None, None),
        P("tower", None, None),
        P("tower", None),
        P(),
        P(("tower", "member"), None),
    )
    return jax.shard_map(
        per_device,
        mesh=mesh,
        in_specs=placed,
        out_specs=(P(("tower", "member"), None), P("tower", None, "member")),
        check_vma=False,
    )
```

```python
import jax
import jax.numpy as jnp
from jax import lax
from jax.experimental import pallas as pl
from jax.experimental.pallas import tpu as pltpu
from jax.sharding import PartitionSpec as P

F32 = jnp.float32
BF16 = jnp.bfloat16
E = 128
N = 4
PUMPS = ((1, 0), (2, 4), (3, 7))
NB = 256
NT = (((1,), (1,)), ((), ()))
TN = (((0,), (0,)), ((), ()))


def dot(a, b):
    return jnp.dot(a, b, preferred_element_type=F32)


def dot_t(a, b):
    return lax.dot_general(a, b, NT, preferred_element_type=F32)


def line_position():
    me = lax.axis_index("member")
    near = me + 1 - 2 * (me % 2)
    hub = ((me + 1) // 2) % 2
    return me, near, 3 - me, hub


class LineSum:
    def __init__(self, block, total, own, mine, from_end, from_side, sems):
        self.me, self.near, self.across, self.hub = line_position()
        self.block, self.total, self.own = block, total, own
        self.mine, self.from_end, self.from_side = mine, from_end, from_side
        self.sems = sems

    def rows(self, c):
        return pl.ds(pl.multiple_of(c * self.block, self.block), self.block)

    def copy(self, kind, src, dst, n, c, peer):
        rows = self.rows(c)
        return pltpu.make_async_remote_copy(
            src_ref=src.at[n, rows],
            dst_ref=dst.at[n, rows],
            send_sem=self.sems.at[2 * kind, n, c],
            recv_sem=self.sems.at[2 * kind + 1, n, c],
            device_id={"member": peer},
        )

    def to_hub(self, n, c):
        return self.copy(0, self.mine, self.from_end, n, c, self.near)

    def to_side(self, n, c):
        return self.copy(1, self.mine, self.from_side, n, c, self.across)

    def to_end(self, n, c):
        return self.copy(2, self.total, self.total, n, c, self.near)

    def put(self, n, c, value):
        @pl.when(self.hub == 1)
        def _():
            self.own[self.rows(c), :] = value

        @pl.when(self.hub == 0)
        def _():
            self.mine[n, self.rows(c), :] = value.astype(BF16)

            @pl.when(c > 0)
            def _():
                self.to_hub(n, c - 1).wait_send()

            self.to_hub(n, c).start()

    def exchange(self, n, c):
        rows = self.rows(c)

        @pl.when(self.hub == 1)
        def _():
            self.to_hub(n, c).wait_recv()
            both = self.own[rows, :] + self.from_end[n, rows, :].astype(F32)
            self.mine[n, rows, :] = both.astype(BF16)
            self.to_side(n, c).start()

    def get(self, n, c):
        rows = self.rows(c)

        @pl.when(self.hub == 1)
        def _():
            self.to_side(n, c).wait_recv()
            whole = self.mine[n, rows, :].astype(F32) + self.from_side[n, rows, :].astype(F32)
            self.total[n, rows, :] = whole.astype(BF16)
            self.to_end(n, c).start()

        @pl.when(self.hub == 0)
        def _():
            self.to_end(n, c).wait_recv()

    def lag(self, hub, end):
        return hub * self.hub + end * (1 - self.hub)

    def drain(self, n):
        @pl.when(self.hub == 1)
        def _():
            def both(c):
                self.to_side(n, c).wait_send()
                self.to_end(n, c).wait_send()

            each(N, both)

        @pl.when(self.hub == 0)
        def _():
            self.to_hub(n, N - 1).wait_send()


def each(count, body, unroll=1):
    lax.fori_loop(0, count, lambda i, _: (body(i), 0)[1], 0, unroll=unroll)


def stage(c, body):
    @pl.when((c >= 0) & (c < N))
    def _():
        body(c)


def ranks(w_ref, k, lo, rows):
    return jnp.concatenate([w_ref[k, r, lo : lo + rows, :] for r in range(N)], axis=1)


def times_down(a, w_ref, k):
    width = w_ref.shape[2]
    halves = []
    for j in range(0, N, 2):
        right = jnp.concatenate([w_ref[k, j], w_ref[k, j + 1]], axis=1)
        halves.append(dot(a, right))
    return jnp.concatenate(halves, axis=1)


def step_kernel(
    inv_ref, owner_ref, x_hbm, down_hbm, up_hbm, bias_ref, proj_hbm, cot_ref,
    out_hbm, inter_ref,
    x_ref, map0, map1, map2, map3, proj_ref, ready, w_ref, pw_ref, bw_ref, cur, scales, grad,
    own, total_ref, mine, from_end, from_side, v_out, v_own, v_in, vg, ordered, got, back, ret,
    bias_slots, picks, cots, tables, out_ref, out_sems,
    load_sems, sems, w_sems, v_sems, g_sems, t_sems,
):
    samples, width = x_ref.shape
    block = samples // N
    rank = N * E
    feats = width // E
    towers, packed, _ = ordered.shape
    vecs, owned, _ = cots.shape
    line = LineSum(block, total_ref, own, mine, from_end, from_side, sems)
    me = line.me
    tower = lax.axis_index("tower")

    def other(d):
        return (tower + 1 + d) % towers

    loads = [
        pltpu.make_async_copy(src, dst, load_sems.at[i])
        for i, (src, dst) in enumerate(
            (
                (down_hbm.at[0], map0),
                (x_hbm, x_ref),
                (up_hbm.at[0], map1),
                (down_hbm.at[1], map2),
                (up_hbm.at[1], map3),
                (proj_hbm, proj_ref),
            )
        )
    ]
    for load in loads:
        load.start()
    barrier = pltpu.get_barrier_semaphore()
    for d in range(1, N):
        pl.semaphore_signal(barrier, inc=1, device_id={"member": (me + d) % N})
    each(towers - 1, lambda d: pl.semaphore_signal(barrier, inc=1, device_id={"tower": other(d)}))

    def send_w(k, d):
        peer = (me + d) % N
        return pltpu.make_async_remote_copy(
            src_ref=ready.at[k, peer],
            dst_ref=w_ref.at[k, me],
            send_sem=w_sems.at[0, k, peer],
            recv_sem=w_sems.at[1, k, me],
            device_id={"member": peer},
        )

    def recv_w(k, d):
        peer = (me + d) % N
        return pltpu.make_async_remote_copy(
            src_ref=ready.at[k, peer],
            dst_ref=w_ref.at[k, peer],
            send_sem=w_sems.at[0, k, peer],
            recv_sem=w_sems.at[1, k, peer],
            device_id={"member": peer},
        )

    def make_ready(k):
        source = (map0, map1, map2, map3)[k]

        def one(f):
            at = pl.multiple_of((f % feats) * E, E)
            ready[k, f // feats, pl.ds(at, E), :] = source[inv_ref[f]]

        each(N * feats, one)
        w_ref[k, me] = ready[k, me]

    def start_w(k):
        for d in range(1, N):
            send_w(k, d).start()

    def sent_w(k):
        for d in range(1, N):
            send_w(k, d).wait_send()

    def got_w(k):
        for d in range(1, N):
            recv_w(k, d).wait_recv()

    def pump(i):
        for k, at in PUMPS:

            @pl.when(i == at)
            def _():
                if k > 1:
                    sent_w(k - 1)
                start_w(k)

    loads[0].wait()
    make_ready(0)
    pl.semaphore_wait(barrier, N - 1 + towers - 1)
    start_w(0)
    for load in loads[1:]:
        load.wait()
    for k in range(1, 4):
        make_ready(k)
    for j in range(N * feats):
        bias_slots[j] = bias_ref[:, j * E : (j + 1) * E]
    for i in range(feats):
        slot = inv_ref[me * feats + i]
        pw_ref[i * E : (i + 1) * E, :] = proj_ref[slot]
        bias = bias_slots[slot]
        for layer in range(2):
            bw_ref[layer, :, i * E : (i + 1) * E] = bias[layer : layer + 1]
    places = lax.broadcasted_iota(jnp.int32, (block, block), 0)
    owns = jnp.where(owner_ref[pl.ds(me, 1), :] == places, 1.0, 0.0).astype(BF16)
    shape = (2 * block, block)
    row = lax.broadcasted_iota(jnp.int32, shape, 0)
    col = lax.broadcasted_iota(jnp.int32, shape, 1)
    for k in range(2):
        spread = jnp.where(row == 2 * col + k, 1.0, 0.0).astype(BF16)
        picks[k] = dot_t(spread, owns).astype(BF16)
    for i in range(vecs):
        cots[i] = cot_ref[:, i * E : (i + 1) * E].astype(F32)
    sent_w(0)
    got_w(0)

    def first_sum(i):
        pump(i)
        stage(i, lambda c: line.put(0, c, times_down(x_ref[line.rows(c), :], w_ref, 0)))
        stage(i, lambda c: line.exchange(0, c))
        stage(i - line.lag(1, 3), lambda c: line.get(0, c))

    each(N + 3, first_sum)
    got_w(1)
    got_w(2)

    def next_current(layer, c):
        rows = line.rows(c)
        hidden = total_ref[layer, rows, :]
        for lo in range(0, width, NB):
            cols = slice(lo, lo + NB)
            scale = dot_t(hidden, ranks(w_ref, 2 * layer + 1, lo, NB)) + bw_ref[layer, :, cols]
            scales[layer, rows, cols] = scale
            x = x_ref[rows, cols].astype(F32)
            before = x if layer == 0 else cur[rows, cols].astype(F32)
            cur[rows, cols] = (x * scale + before).astype(BF16)

    def v_copy(slot, peer):
        return pltpu.make_async_remote_copy(
            src_ref=v_out.at[peer],
            dst_ref=v_in.at[slot],
            send_sem=v_sems.at[0, peer],
            recv_sem=v_sems.at[1, slot],
            device_id={"member": peer},
        )

    def vectors(c):
        next_current(1, c)
        part_v = dot(cur[line.rows(c), :], pw_ref[...])

        @pl.when(c == me)
        def _():
            v_own[...] = part_v

        @pl.when(c != me)
        def _():
            v_out[c] = part_v.astype(BF16)
            v_copy(me, c).start()

    def middle(c):
        next_current(0, c)
        line.put(1, c, times_down(cur[line.rows(c), :], w_ref, 2))

    def second_sum(i):
        pump(N + 3 + i)
        stage(i, middle)
        stage(i, lambda c: line.exchange(1, c))
        stage(i - line.lag(1, 3), lambda c: line.get(1, c))

        @pl.when(i == 3)
        def _():
            got_w(3)

        stage(i - 3, vectors)

    each(N + 3, second_sum)
    vector = v_own[...]
    for d in range(1, N):
        peer = (me + d) % N
        v_copy(peer, peer).wait_recv()
        vector = vector + v_in[peer].astype(F32)
    vector = vector.astype(BF16)
    total = jnp.zeros((2 * block, E), F32)
    for k in range(2):
        total = total + dot(picks[k], vector[:, k * E : (k + 1) * E])
    ordered[...] = total.astype(BF16).reshape(towers, packed, E)

    def swap(phase, src, dst):
        def copy(d):
            return pltpu.make_async_remote_copy(
                src_ref=src.at[other(d)],
                dst_ref=dst.at[tower],
                send_sem=t_sems.at[0, phase],
                recv_sem=t_sems.at[1, phase],
                device_id={"tower": other(d)},
            )

        each(towers - 1, lambda d: copy(d).start(), 9)
        dst[tower] = src[tower]

    def arrived(which, phase, ref):
        all_but_one = ref.at[pl.ds(0, towers - 1)]
        pltpu.make_async_copy(all_but_one, all_but_one, t_sems.at[which, phase]).wait()

    swap(0, ordered, got)
    shape = (vecs, towers * packed)
    row = lax.broadcasted_iota(jnp.int32, shape, 0)
    col = lax.broadcasted_iota(jnp.int32, shape, 1)
    arrived(1, 0, got)
    flat = got[...].reshape(towers * packed, E)
    total = jnp.zeros((towers * packed, E), F32)
    held = []
    for r in range(owned):
        pick = jnp.where(col == (row // 2) * packed + 2 * r + row % 2, 1.0, 0.0).astype(BF16)
        vecs_r = dot(pick, flat).astype(BF16)
        held.append(vecs_r)
        cot = cots[:, r, :].astype(BF16)
        both = dot(cot, vecs_r) + lax.dot_general(cot, vecs_r, TN, preferred_element_type=F32)
        g = (both * (1.0 / E)).astype(BF16)
        total = total + lax.dot_general(pick, g, TN, preferred_element_type=F32)
    back[...] = total.astype(BF16).reshape(towers, packed, E)
    swap(1, back, ret)
    for r in range(owned):
        tables[:, r, :] = dot_t(held[r], held[r]) * (1.0 / E)
    for i in range(vecs):
        inter_ref[:, i * E : (i + 1) * E] = tables[i]
    arrived(1, 1, ret)

    flat = ret[...].reshape(towers * packed, E)
    for k in range(2):
        vg[me, :, k * E : (k + 1) * E] = lax.dot_general(
            picks[k], flat, TN, preferred_element_type=F32
        ).astype(BF16)

    def g_copy(slot, peer):
        return pltpu.make_async_remote_copy(
            src_ref=vg.at[slot],
            dst_ref=vg.at[slot],
            send_sem=g_sems.at[0, peer],
            recv_sem=g_sems.at[1, slot],
            device_id={"member": peer},
        )

    for d in range(1, N):
        g_copy(me, (me + d) % N).start()

    def last_layer(c):
        rows = line.rows(c)

        @pl.when(c != me)
        def _():
            g_copy(c, c).wait_recv()

        total = jnp.zeros((block, rank), F32)
        for lo in range(0, width, NB):
            cols = slice(lo, lo + NB)
            g = dot_t(vg[c], pw_ref[cols, :])
            grad[rows, cols] = g
            dscale = (g * x_ref[rows, cols].astype(F32)).astype(BF16)
            total = total + dot(dscale, ranks(w_ref, 3, lo, NB))
        line.put(2, c, total)

    def first_layer(c):
        rows = line.rows(c)
        line.get(2, c)
        dhidden = total_ref[2, rows, :]
        total = jnp.zeros((block, rank), F32)
        for lo in range(0, width, NB):
            cols = slice(lo, lo + NB)
            g2 = grad[rows, cols]
            g1 = g2 + dot_t(dhidden, ranks(w_ref, 2, lo, NB))
            grad[rows, cols] = g1 + (g2 * scales[1, rows, cols] + g1 * scales[0, rows, cols])
            dscale = (g1 * x_ref[rows, cols].astype(F32)).astype(BF16)
            total = total + dot(dscale, ranks(w_ref, 1, lo, NB))
        line.put(3, c, total)

    def out_copy(c):
        rows = line.rows(c)
        return pltpu.make_async_copy(out_ref.at[rows], out_hbm.at[rows], out_sems.at[c])

    def finish(c):
        rows = line.rows(c)
        line.get(3, c)
        dhidden = total_ref[3, rows, :]
        for lo in range(0, width, NB):
            cols = slice(lo, lo + NB)
            g0 = grad[rows, cols] + dot_t(dhidden, ranks(w_ref, 0, lo, NB))
            out_ref[rows, cols] = g0.astype(BF16)
        out_copy(c).start()

    def both_sums(i):
        stage(i, last_layer)
        stage(i, lambda c: line.exchange(2, c))
        stage(i - line.lag(1, 3), first_layer)
        stage(i - 3, lambda c: line.exchange(3, c))
        stage(i - line.lag(4, 6), finish)

    each(N + 6, both_sums)

    each(N, lambda c: out_copy(c).wait())
    sent_w(3)
    for d in range(1, N):
        v_copy(me, (me + d) % N).wait_send()
        g_copy(me, (me + d) % N).wait_send()
    for phase in range(2):
        arrived(0, phase, got)
    for n in range(4):
        line.drain(n)


def vmem():
    return pl.BlockSpec(memory_space=pltpu.VMEM)


def params(collective_id):
    return pltpu.CompilerParams(
        collective_id=collective_id, has_side_effects=True, vmem_limit_bytes=60 << 20
    )


def per_device(slabs, cross_down, cross_up, cross_bias, projector, placement, owner, inter_grad):
    x = slabs[0]
    samples, width = x.shape
    block = samples // N
    slots = placement.shape[1]
    rank = N * cross_down.shape[3]
    towers = block // 4
    order = placement[0]
    index = jnp.arange(slots, dtype=jnp.int32)
    inverse = jnp.sum(jnp.where(order[None, :] == index[:, None], index[None, :], 0), axis=1)
    sds = jax.ShapeDtypeStruct
    dma = pltpu.SemaphoreType.DMA
    any_spec = pl.BlockSpec(memory_space=pl.ANY)
    slab_grad, interactions = pl.pallas_call(
        step_kernel,
        out_shape=(sds((samples, width), BF16), sds(inter_grad.shape, F32)),
        in_specs=[
            pl.BlockSpec(memory_space=pltpu.SMEM), vmem(), any_spec, any_spec, any_spec,
            vmem(), any_spec, vmem(),
        ],
        out_specs=(any_spec, vmem()),
        scratch_shapes=[
            pltpu.VMEM((samples, width), BF16),
            *[pltpu.VMEM((slots, E, E), BF16)] * 4,
            pltpu.VMEM((slots, E, 2 * E), BF16),
            pltpu.VMEM((4, N, width, E), BF16),
            pltpu.VMEM((4, N, width, E), BF16),
            pltpu.VMEM((width, 2 * E), BF16),
            pltpu.VMEM((2, 1, width), F32),
            pltpu.VMEM((samples, width), BF16),
            pltpu.VMEM((2, samples, width), F32),
            pltpu.VMEM((samples, width), F32),
            pltpu.VMEM((samples, rank), F32),
            *[pltpu.VMEM((4, samples, rank), BF16)] * 4,
            pltpu.VMEM((N, block, 2 * E), BF16),
            pltpu.VMEM((block, 2 * E), F32),
            pltpu.VMEM((N, block, 2 * E), BF16),
            pltpu.VMEM((N, block, 2 * E), BF16),
            *[pltpu.VMEM((towers, 8, E), BF16)] * 4,
            pltpu.VMEM((slots, 2, E), F32),
            pltpu.VMEM((2, 2 * block, block), BF16),
            *[pltpu.VMEM((2 * towers, inter_grad.shape[0], E), F32)] * 2,
            pltpu.VMEM((samples, width), BF16),
            dma((N,)),
            dma((6,)),
            dma((6, 4, N)),
            dma((2, 4, N)),
            dma((2, N)),
            dma((2, N)),
            dma((2, 2)),
        ],
        compiler_params=params(0),
        name="mega",
    )(
        inverse, owner, x,
        cross_down[0].reshape(2, slots, E, E), cross_up[0].reshape(2, slots, E, E),
        cross_bias[0], projector[0].reshape(slots, E, 2 * E), inter_grad,
    )
    return interactions, slab_grad[None]


def solution(mesh):
    placed = (
        P("tower", None, "member"),
        P("tower", None, None, "member"),
        P("tower", None, None, "member"),
        P("tower", None, None),
        P("tower", None, None),
        P("tower", None),
        P(),
        P(("tower", "member"), None),
    )
    return jax.shard_map(
        per_device,
        mesh=mesh,
        in_specs=placed,
        out_specs=(P(("tower", "member"), None), P("tower", None, "member")),
        check_vma=False,
    )
```

```python
import jax
import jax.numpy as jnp
from jax import lax
from jax.experimental import pallas as pl
from jax.experimental.pallas import tpu as pltpu
from jax.sharding import PartitionSpec as P

F32 = jnp.float32
BF16 = jnp.bfloat16
E = 128
N = 4
PUMPS = ((1, 0), (2, 4), (3, 7))
NB = 512
NT = (((1,), (1,)), ((), ()))
TN = (((0,), (0,)), ((), ()))


def dot(a, b):
    return jnp.dot(a, b, preferred_element_type=F32)


def dot_t(a, b):
    return lax.dot_general(a, b, NT, preferred_element_type=F32)


def line_position():
    me = lax.axis_index("member")
    near = me + 1 - 2 * (me % 2)
    hub = ((me + 1) // 2) % 2
    return me, near, 3 - me, hub


class LineSum:
    def __init__(self, block, total, own, mine, from_end, from_side, sems):
        self.me, self.near, self.across, self.hub = line_position()
        self.block, self.total, self.own = block, total, own
        self.mine, self.from_end, self.from_side = mine, from_end, from_side
        self.sems = sems

    def rows(self, c):
        return pl.ds(pl.multiple_of(c * self.block, self.block), self.block)

    def copy(self, kind, src, dst, n, c, peer):
        rows = self.rows(c)
        return pltpu.make_async_remote_copy(
            src_ref=src.at[n, rows],
            dst_ref=dst.at[n, rows],
            send_sem=self.sems.at[2 * kind, n, c],
            recv_sem=self.sems.at[2 * kind + 1, n, c],
            device_id={"member": peer},
        )

    def to_hub(self, n, c):
        return self.copy(0, self.mine, self.from_end, n, c, self.near)

    def to_side(self, n, c):
        return self.copy(1, self.mine, self.from_side, n, c, self.across)

    def to_end(self, n, c):
        return self.copy(2, self.total, self.total, n, c, self.near)

    def put(self, n, c, value):
        @pl.when(self.hub == 1)
        def _():
            self.own[self.rows(c), :] = value

        @pl.when(self.hub == 0)
        def _():
            self.mine[n, self.rows(c), :] = value.astype(BF16)

            @pl.when(c > 0)
            def _():
                self.to_hub(n, c - 1).wait_send()

            self.to_hub(n, c).start()

    def exchange(self, n, c):
        rows = self.rows(c)

        @pl.when(self.hub == 1)
        def _():
            self.to_hub(n, c).wait_recv()
            both = self.own[rows, :] + self.from_end[n, rows, :].astype(F32)
            self.mine[n, rows, :] = both.astype(BF16)
            self.to_side(n, c).start()

    def get(self, n, c):
        rows = self.rows(c)

        @pl.when(self.hub == 1)
        def _():
            self.to_side(n, c).wait_recv()
            whole = self.mine[n, rows, :].astype(F32) + self.from_side[n, rows, :].astype(F32)
            self.total[n, rows, :] = whole.astype(BF16)
            self.to_end(n, c).start()

        @pl.when(self.hub == 0)
        def _():
            self.to_end(n, c).wait_recv()

    def lag(self, hub, end):
        return hub * self.hub + end * (1 - self.hub)

    def drain(self, n):
        @pl.when(self.hub == 1)
        def _():
            def both(c):
                self.to_side(n, c).wait_send()
                self.to_end(n, c).wait_send()

            each(N, both)

        @pl.when(self.hub == 0)
        def _():
            self.to_hub(n, N - 1).wait_send()


def each(count, body, unroll=1):
    lax.fori_loop(0, count, lambda i, _: (body(i), 0)[1], 0, unroll=unroll)


def stage(c, body):
    @pl.when((c >= 0) & (c < N))
    def _():
        body(c)


def ranks(w_ref, k, lo, rows):
    return jnp.concatenate([w_ref[k, r, lo : lo + rows, :] for r in range(N)], axis=1)


def times_down(a, w_ref, k):
    width = w_ref.shape[2]
    halves = []
    for j in range(0, N, 2):
        right = jnp.concatenate([w_ref[k, j], w_ref[k, j + 1]], axis=1)
        halves.append(dot(a, right))
    return jnp.concatenate(halves, axis=1)


def step_kernel(
    inv_ref, owner_ref, x_hbm, down_hbm, up_hbm, bias_ref, proj_hbm, cot_ref,
    out_hbm, inter_ref,
    x_ref, map0, map1, map2, map3, proj_ref, ready, w_ref, pw_ref, bw_ref, cur, scales, grad,
    own, total_ref, mine, from_end, from_side, v_out, v_own, v_in, vg, ordered, got, back, ret,
    bias_slots, picks, cots, tables, out_ref, out_sems,
    load_sems, sems, w_sems, v_sems, g_sems, t_sems,
):
    samples, width = x_ref.shape
    block = samples // N
    rank = N * E
    feats = width // E
    towers, packed, _ = ordered.shape
    vecs, owned, _ = cots.shape
    line = LineSum(block, total_ref, own, mine, from_end, from_side, sems)
    me = line.me
    tower = lax.axis_index("tower")

    def other(d):
        return (tower + 1 + d) % towers

    loads = [
        pltpu.make_async_copy(src, dst, load_sems.at[i])
        for i, (src, dst) in enumerate(
            (
                (down_hbm.at[0], map0),
                (x_hbm, x_ref),
                (up_hbm.at[0], map1),
                (down_hbm.at[1], map2),
                (up_hbm.at[1], map3),
                (proj_hbm, proj_ref),
            )
        )
    ]
    for load in loads:
        load.start()
    barrier = pltpu.get_barrier_semaphore()
    for d in range(1, N):
        pl.semaphore_signal(barrier, inc=1, device_id={"member": (me + d) % N})
    each(towers - 1, lambda d: pl.semaphore_signal(barrier, inc=1, device_id={"tower": other(d)}))

    def send_w(k, d):
        peer = (me + d) % N
        return pltpu.make_async_remote_copy(
            src_ref=ready.at[k, peer],
            dst_ref=w_ref.at[k, me],
            send_sem=w_sems.at[0, k, peer],
            recv_sem=w_sems.at[1, k, me],
            device_id={"member": peer},
        )

    def recv_w(k, d):
        peer = (me + d) % N
        return pltpu.make_async_remote_copy(
            src_ref=ready.at[k, peer],
            dst_ref=w_ref.at[k, peer],
            send_sem=w_sems.at[0, k, peer],
            recv_sem=w_sems.at[1, k, peer],
            device_id={"member": peer},
        )

    def make_ready(k):
        source = (map0, map1, map2, map3)[k]

        def one(f):
            at = pl.multiple_of((f % feats) * E, E)
            ready[k, f // feats, pl.ds(at, E), :] = source[inv_ref[f]]

        each(N * feats, one)
        w_ref[k, me] = ready[k, me]

    def start_w(k):
        for d in range(1, N):
            send_w(k, d).start()

    def sent_w(k):
        for d in range(1, N):
            send_w(k, d).wait_send()

    def got_w(k):
        for d in range(1, N):
            recv_w(k, d).wait_recv()

    def pump(i):
        for k, at in PUMPS:

            @pl.when(i == at)
            def _():
                if k > 1:
                    sent_w(k - 1)
                start_w(k)

    loads[0].wait()
    make_ready(0)
    pl.semaphore_wait(barrier, N - 1 + towers - 1)
    start_w(0)
    for load in loads[1:]:
        load.wait()
    for k in range(1, 4):
        make_ready(k)
    for j in range(N * feats):
        bias_slots[j] = bias_ref[:, j * E : (j + 1) * E]
    for i in range(feats):
        slot = inv_ref[me * feats + i]
        pw_ref[i * E : (i + 1) * E, :] = proj_ref[slot]
        bias = bias_slots[slot]
        for layer in range(2):
            bw_ref[layer, :, i * E : (i + 1) * E] = bias[layer : layer + 1]
    places = lax.broadcasted_iota(jnp.int32, (block, block), 0)
    owns = jnp.where(owner_ref[pl.ds(me, 1), :] == places, 1.0, 0.0).astype(BF16)
    shape = (2 * block, block)
    row = lax.broadcasted_iota(jnp.int32, shape, 0)
    col = lax.broadcasted_iota(jnp.int32, shape, 1)
    for k in range(2):
        spread = jnp.where(row == 2 * col + k, 1.0, 0.0).astype(BF16)
        picks[k] = dot_t(spread, owns).astype(BF16)
    for i in range(vecs):
        cots[i] = cot_ref[:, i * E : (i + 1) * E].astype(F32)
    sent_w(0)
    got_w(0)

    def first_sum(i):
        pump(i)
        stage(i, lambda c: line.put(0, c, times_down(x_ref[line.rows(c), :], w_ref, 0)))
        stage(i, lambda c: line.exchange(0, c))
        stage(i - line.lag(1, 3), lambda c: line.get(0, c))

    each(N + 3, first_sum)
    got_w(1)
    got_w(2)

    def next_current(layer, c):
        rows = line.rows(c)
        hidden = total_ref[layer, rows, :]
        for lo in range(0, width, NB):
            cols = slice(lo, lo + NB)
            scale = dot_t(hidden, ranks(w_ref, 2 * layer + 1, lo, NB)) + bw_ref[layer, :, cols]
            scales[layer, rows, cols] = scale
            x = x_ref[rows, cols].astype(F32)
            before = x if layer == 0 else cur[rows, cols].astype(F32)
            cur[rows, cols] = (x * scale + before).astype(BF16)

    def v_copy(slot, peer):
        return pltpu.make_async_remote_copy(
            src_ref=v_out.at[peer],
            dst_ref=v_in.at[slot],
            send_sem=v_sems.at[0, peer],
            recv_sem=v_sems.at[1, slot],
            device_id={"member": peer},
        )

    def vectors(c):
        next_current(1, c)
        part_v = dot(cur[line.rows(c), :], pw_ref[...])

        @pl.when(c == me)
        def _():
            v_own[...] = part_v

        @pl.when(c != me)
        def _():
            v_out[c] = part_v.astype(BF16)
            v_copy(me, c).start()

    def middle(c):
        next_current(0, c)
        line.put(1, c, times_down(cur[line.rows(c), :], w_ref, 2))

    def second_sum(i):
        pump(N + 3 + i)
        stage(i, middle)
        stage(i, lambda c: line.exchange(1, c))
        stage(i - line.lag(1, 3), lambda c: line.get(1, c))

        @pl.when(i == 3)
        def _():
            got_w(3)

        stage(i - 3, vectors)

    each(N + 3, second_sum)
    vector = v_own[...]
    for d in range(1, N):
        peer = (me + d) % N
        v_copy(peer, peer).wait_recv()
        vector = vector + v_in[peer].astype(F32)
    vector = vector.astype(BF16)
    total = jnp.zeros((2 * block, E), F32)
    for k in range(2):
        total = total + dot(picks[k], vector[:, k * E : (k + 1) * E])
    ordered[...] = total.astype(BF16).reshape(towers, packed, E)

    def swap(phase, src, dst):
        def copy(d):
            return pltpu.make_async_remote_copy(
                src_ref=src.at[other(d)],
                dst_ref=dst.at[tower],
                send_sem=t_sems.at[0, phase],
                recv_sem=t_sems.at[1, phase],
                device_id={"tower": other(d)},
            )

        each(towers - 1, lambda d: copy(d).start(), 9)
        dst[tower] = src[tower]

    def arrived(which, phase, ref):
        all_but_one = ref.at[pl.ds(0, towers - 1)]
        pltpu.make_async_copy(all_but_one, all_but_one, t_sems.at[which, phase]).wait()

    swap(0, ordered, got)
    shape = (vecs, towers * packed)
    row = lax.broadcasted_iota(jnp.int32, shape, 0)
    col = lax.broadcasted_iota(jnp.int32, shape, 1)
    arrived(1, 0, got)
    flat = got[...].reshape(towers * packed, E)
    total = jnp.zeros((towers * packed, E), F32)
    held = []
    for r in range(owned):
        pick = jnp.where(col == (row // 2) * packed + 2 * r + row % 2, 1.0, 0.0).astype(BF16)
        vecs_r = dot(pick, flat).astype(BF16)
        held.append(vecs_r)
        cot = cots[:, r, :].astype(BF16)
        both = dot(cot, vecs_r) + lax.dot_general(cot, vecs_r, TN, preferred_element_type=F32)
        g = (both * (1.0 / E)).astype(BF16)
        total = total + lax.dot_general(pick, g, TN, preferred_element_type=F32)
    back[...] = total.astype(BF16).reshape(towers, packed, E)
    swap(1, back, ret)
    for r in range(owned):
        tables[:, r, :] = dot_t(held[r], held[r]) * (1.0 / E)
    for i in range(vecs):
        inter_ref[:, i * E : (i + 1) * E] = tables[i]
    arrived(1, 1, ret)

    flat = ret[...].reshape(towers * packed, E)
    for k in range(2):
        vg[me, :, k * E : (k + 1) * E] = lax.dot_general(
            picks[k], flat, TN, preferred_element_type=F32
        ).astype(BF16)

    def g_copy(slot, peer):
        return pltpu.make_async_remote_copy(
            src_ref=vg.at[slot],
            dst_ref=vg.at[slot],
            send_sem=g_sems.at[0, peer],
            recv_sem=g_sems.at[1, slot],
            device_id={"member": peer},
        )

    for d in range(1, N):
        g_copy(me, (me + d) % N).start()

    def last_layer(c):
        rows = line.rows(c)

        @pl.when(c != me)
        def _():
            g_copy(c, c).wait_recv()

        total = jnp.zeros((block, rank), F32)
        for lo in range(0, width, NB):
            cols = slice(lo, lo + NB)
            g = dot_t(vg[c], pw_ref[cols, :])
            grad[rows, cols] = g
            dscale = (g * x_ref[rows, cols].astype(F32)).astype(BF16)
            total = total + dot(dscale, ranks(w_ref, 3, lo, NB))
        line.put(2, c, total)

    def first_layer(c):
        rows = line.rows(c)
        line.get(2, c)
        dhidden = total_ref[2, rows, :]
        total = jnp.zeros((block, rank), F32)
        for lo in range(0, width, NB):
            cols = slice(lo, lo + NB)
            g2 = grad[rows, cols]
            g1 = g2 + dot_t(dhidden, ranks(w_ref, 2, lo, NB))
            grad[rows, cols] = g1 + (g2 * scales[1, rows, cols] + g1 * scales[0, rows, cols])
            dscale = (g1 * x_ref[rows, cols].astype(F32)).astype(BF16)
            total = total + dot(dscale, ranks(w_ref, 1, lo, NB))
        line.put(3, c, total)

    def out_copy(c):
        rows = line.rows(c)
        return pltpu.make_async_copy(out_ref.at[rows], out_hbm.at[rows], out_sems.at[c])

    def finish(c):
        rows = line.rows(c)
        line.get(3, c)
        dhidden = total_ref[3, rows, :]
        for lo in range(0, width, NB):
            cols = slice(lo, lo + NB)
            g0 = grad[rows, cols] + dot_t(dhidden, ranks(w_ref, 0, lo, NB))
            out_ref[rows, cols] = g0.astype(BF16)
        out_copy(c).start()

    def both_sums(i):
        stage(i, last_layer)
        stage(i, lambda c: line.exchange(2, c))
        stage(i - line.lag(1, 3), first_layer)
        stage(i - 3, lambda c: line.exchange(3, c))
        stage(i - line.lag(4, 6), finish)

    each(N + 6, both_sums)

    each(N, lambda c: out_copy(c).wait())
    sent_w(3)
    for d in range(1, N):
        v_copy(me, (me + d) % N).wait_send()
        g_copy(me, (me + d) % N).wait_send()
    for phase in range(2):
        arrived(0, phase, got)
    for n in range(4):
        line.drain(n)


def vmem():
    return pl.BlockSpec(memory_space=pltpu.VMEM)


def params(collective_id):
    return pltpu.CompilerParams(
        collective_id=collective_id, has_side_effects=True, vmem_limit_bytes=60 << 20
    )


def per_device(slabs, cross_down, cross_up, cross_bias, projector, placement, owner, inter_grad):
    x = slabs[0]
    samples, width = x.shape
    block = samples // N
    slots = placement.shape[1]
    rank = N * cross_down.shape[3]
    towers = block // 4
    order = placement[0]
    index = jnp.arange(slots, dtype=jnp.int32)
    inverse = jnp.sum(jnp.where(order[None, :] == index[:, None], index[None, :], 0), axis=1)
    sds = jax.ShapeDtypeStruct
    dma = pltpu.SemaphoreType.DMA
    any_spec = pl.BlockSpec(memory_space=pl.ANY)
    slab_grad, interactions = pl.pallas_call(
        step_kernel,
        out_shape=(sds((samples, width), BF16), sds(inter_grad.shape, F32)),
        in_specs=[
            pl.BlockSpec(memory_space=pltpu.SMEM), vmem(), any_spec, any_spec, any_spec,
            vmem(), any_spec, vmem(),
        ],
        out_specs=(any_spec, vmem()),
        scratch_shapes=[
            pltpu.VMEM((samples, width), BF16),
            *[pltpu.VMEM((slots, E, E), BF16)] * 4,
            pltpu.VMEM((slots, E, 2 * E), BF16),
            pltpu.VMEM((4, N, width, E), BF16),
            pltpu.VMEM((4, N, width, E), BF16),
            pltpu.VMEM((width, 2 * E), BF16),
            pltpu.VMEM((2, 1, width), F32),
            pltpu.VMEM((samples, width), BF16),
            pltpu.VMEM((2, samples, width), F32),
            pltpu.VMEM((samples, width), F32),
            pltpu.VMEM((samples, rank), F32),
            *[pltpu.VMEM((4, samples, rank), BF16)] * 4,
            pltpu.VMEM((N, block, 2 * E), BF16),
            pltpu.VMEM((block, 2 * E), F32),
            pltpu.VMEM((N, block, 2 * E), BF16),
            pltpu.VMEM((N, block, 2 * E), BF16),
            *[pltpu.VMEM((towers, 8, E), BF16)] * 4,
            pltpu.VMEM((slots, 2, E), F32),
            pltpu.VMEM((2, 2 * block, block), BF16),
            *[pltpu.VMEM((2 * towers, inter_grad.shape[0], E), F32)] * 2,
            pltpu.VMEM((samples, width), BF16),
            dma((N,)),
            dma((6,)),
            dma((6, 4, N)),
            dma((2, 4, N)),
            dma((2, N)),
            dma((2, N)),
            dma((2, 2)),
        ],
        compiler_params=params(0),
        name="mega",
    )(
        inverse, owner, x,
        cross_down[0].reshape(2, slots, E, E), cross_up[0].reshape(2, slots, E, E),
        cross_bias[0], projector[0].reshape(slots, E, 2 * E), inter_grad,
    )
    return interactions, slab_grad[None]


def solution(mesh):
    placed = (
        P("tower", None, "member"),
        P("tower", None, None, "member"),
        P("tower", None, None, "member"),
        P("tower", None, None),
        P("tower", None, None),
        P("tower", None),
        P(),
        P(("tower", "member"), None),
    )
    return jax.shard_map(
        per_device,
        mesh=mesh,
        in_specs=placed,
        out_specs=(P(("tower", "member"), None), P("tower", None, "member")),
        check_vma=False,
    )
```
